32 devices in a mesh: row: 16 (over z, x, core), col: 2 (over y).
Axes of the slice: x: 2, y: 2, z: 4, core: 2. Of those that a mesh axis runs over, the one named last changes fastest.
Arguments:
- contact_map: bfloat16 [64, 512, 512], P(None, 'row', 'col'), may hold values from -6 to 6
- dilations: int32 [3], replicated, may hold values from 1 to 8, as said below
- conv_weight: bfloat16 [3, 9, 32, 64], replicated, may hold values from -0.25 to 0.25
- conv_gain: float32 [3, 32], replicated, may hold values from 0.5 to 2
- conv_shift: float32 [3, 32], replicated, may hold values from -0.5 to 0.5
- out_weight: bfloat16 [3, 64, 32], replicated, may hold values from -1 to 1
Outputs:
- contact_out: bfloat16 [64, 512, 512], P(None, 'row', 'col')
The draws below stay inside these ranges and needn't reach their ends.
Inputs may be any that keep to these rules, and one draw needn't show every extreme that they name: `dilations`: each block's dilation; some block's dilation equals 8.
All inputs are finite; a program needn't handle non-finite values.
Results may differ from the reference program's by a relative error of at most 0.0071.
Values may be sent and summed in bfloat16 or wider, within the bound.
A program may use at most 64 MiB of HBM per device.

```python
import math
import jax
import jax.numpy as jnp
from jax import lax

C = 64
HID = 32
DMAX = 8
BLOCKS = 3
BR = 32
N = 512
N_ROW = 16


def draw_dilations(key, part):
    rate_key = jax.random.fold_in(key, 11)
    chosen_key = jax.random.fold_in(key, 23)
    dilation_rates = jax.random.randint(rate_key, (BLOCKS,), 1, DMAX + 1, dtype=jnp.int32)
    chosen = jax.random.randint(chosen_key, (), 0, BLOCKS, dtype=jnp.int32)
    positions = jnp.arange(BLOCKS, dtype=jnp.int32)
    return jnp.where(positions == chosen, DMAX, dilation_rates).astype(jnp.int32)


def shard_levels(key, extent, cuts, least, top_value):
    def one(position, parts):
        heights = jax.random.uniform(jax.random.fold_in(jax.random.fold_in(key, 6), position), (parts,), jnp.float32, least / len(cuts), top_value / len(cuts))
        return jnp.repeat(jnp.exp(heights), extent[position] // parts).reshape((-1,) + (1,) * (len(extent) - position - 1))

    loudness = one(*cuts[0])
    for cut in cuts[1:]:
        loudness = loudness * one(*cut)
    return loudness


def noise(stream_key, extent, deviation, most, shards=(), kind=jnp.bfloat16):
    result = jax.random.normal(stream_key, extent, jnp.float32) * deviation
    if len(shards) > 0:
        result = shard_levels(stream_key, extent, shards, -0.22, 0.18) * result
    return jnp.clip(result, min=-most, max=most).astype(kind)


def setup_inputs(seed: int = 0) -> dict:
    seeds = jax.random.split(jax.random.key(seed), 7)
    contact_map = noise(seeds[0], (C, N, N), 1.0, 6.0, ((1, 16), (2, 2)))
    dilations = draw_dilations(jax.random.fold_in(seeds[6], 71), 0)
    conv_weight = noise(seeds[2], (BLOCKS, 9, HID, C), (9 * C) ** -0.5, 0.25)
    conv_gain = jnp.clip(jnp.exp(jax.random.uniform(seeds[3], (BLOCKS, HID), jnp.float32, math.log(0.5), math.log(2.0))), 0.5, 2.0)
    conv_shift = jnp.clip(jax.random.uniform(seeds[4], (BLOCKS, HID), jnp.float32, -0.5, 0.5), -0.5, 0.5)
    out_weight = noise(seeds[5], (BLOCKS, C, HID), HID ** -0.5, 1.0)
    return dict(contact_map=contact_map, dilations=dilations, conv_weight=conv_weight, conv_gain=conv_gain, conv_shift=conv_shift, out_weight=out_weight)


def residual_block(feature_map, dilations, conv_weight, conv_gain, conv_shift, out_weight, layer_index):
    active = jnp.maximum(feature_map, jnp.zeros((), feature_map.dtype))
    padded = jnp.pad(active, ((0, 0), (DMAX, DMAX), (DMAX, DMAX)))
    spacing = dilations[layer_index].astype(jnp.int32)
    zero_start = jnp.zeros((), jnp.int32)
    kernel = conv_weight[layer_index].astype(jnp.float32)
    expand = out_weight[layer_index].astype(jnp.float32)
    gain_col = conv_gain[layer_index].astype(jnp.float32)[:, None, None]
    shift_col = conv_shift[layer_index].astype(jnp.float32)[:, None, None]

    def stripe(number):
        top_row = (number * BR).astype(jnp.int32)
        band_rows = lax.dynamic_slice(padded, (zero_start, top_row, zero_start), (C, BR + 2 * DMAX, N + 2 * DMAX))
        accumulated = jnp.zeros((HID, BR, N), jnp.float32)
        for offset_row in range(3):
            for offset_col in range(3):
                row_start = (DMAX + (offset_row - 1) * spacing).astype(jnp.int32)
                col_start = (DMAX + (offset_col - 1) * spacing).astype(jnp.int32)
                window = lax.dynamic_slice(band_rows, (zero_start, row_start, col_start), (C, BR, N))
                accumulated = accumulated + jnp.einsum("oc,cyx->oyx", kernel[3 * offset_row + offset_col], window.astype(jnp.float32))
        hidden = jnp.maximum(gain_col * accumulated + shift_col, 0.0).astype(jnp.bfloat16)
        center = lax.dynamic_slice(feature_map, (zero_start, top_row, zero_start), (C, BR, N))
        updated = center.astype(jnp.float32) + jnp.einsum("oh,hyx->oyx", expand, hidden.astype(jnp.float32))
        return updated.astype(jnp.bfloat16)

    stripes = lax.map(stripe, jnp.arange(N_ROW, dtype=jnp.int32))
    return jnp.transpose(stripes, (1, 0, 2, 3)).reshape(C, N, N)


def reference(contact_map, dilations, conv_weight, conv_gain, conv_shift, out_weight):
    feature_map = contact_map
    for layer_index in range(BLOCKS):
        if layer_index == 2:
            mirrored = jnp.swapaxes(feature_map, 1, 2)
            feature_map = (0.5 * (feature_map.astype(jnp.float32) + mirrored.astype(jnp.float32))).astype(jnp.bfloat16)
        feature_map = residual_block(feature_map, dilations, conv_weight, conv_gain, conv_shift, out_weight, layer_index)
    return feature_map
```

```python
import functools

import jax
import jax.numpy as jnp
from jax import lax
from jax.experimental import pallas as pl
from jax.experimental.pallas import tpu as pltpu
from jax.sharding import PartitionSpec as P

DMAX = 8
LANES = 128
F32 = jnp.float32
BF16 = jnp.bfloat16
VMEM_SPEC = pl.BlockSpec(memory_space=pltpu.VMEM)
SMEM_SPEC = pl.BlockSpec(memory_space=pltpu.SMEM)


def row_rim(shard, width):
    count, length = lax.axis_size("row"), shard.shape[1]
    up = [(i, (i + 1) % count) for i in range(count - 1)]
    down = [(j, i) for i, j in up]
    before = lax.ppermute(shard[:, length - width :], "row", up)
    after = lax.ppermute(shard[:, :width], "row", down)
    return jnp.concatenate([before, shard, after], axis=1)


def col_rim(shard, width):
    count, length = lax.axis_size("col"), shard.shape[2]
    up = [(i, (i + 1) % count) for i in range(count - 1)]
    down = [(j, i) for i, j in up]
    before = lax.ppermute(shard[:, :, length - width :], "col", up)
    after = lax.ppermute(shard[:, :, :width], "col", down)
    gap = jnp.zeros(shard.shape[:2] + (LANES - 2 * width,), shard.dtype)
    return jnp.concatenate([shard, after, gap, before], axis=2)


def conv_row(src_ref, i, s, w, gain, shift, expand):
    zero = jnp.zeros((), BF16)
    width = src_ref.shape[2]
    hid = gain.shape[0]
    center = src_ref[i + DMAX]
    stacked = jnp.concatenate(
        [src_ref[i + DMAX - s], center, src_ref[i + DMAX + s]], axis=0
    )
    taps = jnp.dot(w, jnp.maximum(stacked, zero), preferred_element_type=F32)
    conv = (
        pltpu.roll(taps[:hid], s, 1)
        + taps[hid : 2 * hid]
        + pltpu.roll(taps[2 * hid :], width - s, 1)
    )
    hidden = jnp.maximum(gain * conv + shift, 0.0).astype(BF16)
    return center.astype(F32) + jnp.dot(expand, hidden, preferred_element_type=F32)


def spread(x_ref, wide, by_row, rows):
    channels = x_ref.shape[0] // rows

    @pl.loop(0, channels)
    def _(c):
        start = pl.multiple_of(c * rows, rows)
        for g in range(wide.shape[0]):
            wide[g, pl.ds(start, rows), :] = x_ref[
                pl.ds(start, rows), g * LANES : (g + 1) * LANES
            ].astype(F32)

    @pl.loop(0, rows)
    def _(i):
        for g in range(wide.shape[0]):
            by_row[i, :, g * LANES : (g + 1) * LANES] = wide[
                g, pl.ds(i, channels, stride=rows), :
            ].astype(BF16)


def first_kernel(
    tile_rows, tile_cols, dil, x_ref, w_ref, gain_ref, shift_ref, expand_ref,
    f2_ref, turned_ref, wide, by_row, first, second
):
    deep_rows = tile_rows + 4 * DMAX
    mid_rows = tile_rows + 2 * DMAX
    width = x_ref.shape[1]
    channels = expand_ref.shape[1]
    spread(x_ref, wide, by_row, deep_rows)
    row_base = lax.axis_index("row") * tile_rows - DMAX
    total_rows = lax.axis_size("row") * tile_rows
    lane = lax.broadcasted_iota(jnp.int32, (channels, width), 1)
    col = lax.axis_index("col") * tile_cols + jnp.where(lane < tile_cols + LANES // 2, lane, lane - width)
    col_inside = (col >= 0) & (col < lax.axis_size("col") * tile_cols)
    col_mask = jnp.where(col_inside, 1.0, 0.0).astype(F32)

    s0 = dil[0]

    @pl.loop(0, mid_rows, unroll=2)
    def _(i):
        value = conv_row(by_row, i, s0, w_ref[0], gain_ref[0], shift_ref[0], expand_ref[0])
        row = row_base + i
        inside = jnp.where((row >= 0) & (row < total_rows), 1.0, 0.0).astype(F32)
        first[i] = (value * (col_mask * inside)).astype(BF16)

    s1 = dil[1]

    @pl.loop(0, tile_rows, unroll=2)
    def _(i):
        value = conv_row(first, i, s1, w_ref[1], gain_ref[1], shift_ref[1], expand_ref[1])
        for g in range(second.shape[0]):
            second[g, pl.ds(i, channels, stride=tile_rows), :] = value[
                :, g * LANES : (g + 1) * LANES
            ]

    for chunk in range(channels * tile_rows // LANES):
        at = slice(chunk * LANES, (chunk + 1) * LANES)
        for g in range(second.shape[0]):
            across = slice(g * LANES, (g + 1) * LANES)
            block = second[g, at, :]
            f2_ref[at, across] = block.astype(BF16)
            turned_ref[across, at] = block.T.astype(BF16)


def last_kernel(
    tile_rows, tile_cols, dil, x_ref, w_ref, gain_ref, shift_ref, expand_ref,
    out_ref, wide, by_row, second
):
    channels = expand_ref.shape[1]
    spread(x_ref, wide, by_row, tile_rows + 2 * DMAX)
    s = dil[2]

    @pl.loop(0, tile_rows, unroll=2)
    def _(i):
        value = conv_row(by_row, i, s, w_ref[2], gain_ref[2], shift_ref[2], expand_ref[2])
        for g in range(second.shape[0]):
            second[g, pl.ds(i, channels, stride=tile_rows), :] = value[
                :, g * LANES : (g + 1) * LANES
            ]

    for g in range(second.shape[0]):
        out_ref[:, g * LANES : (g + 1) * LANES] = second[g].astype(BF16)


def exchange_kernel(group, sent, got, send_sem, recv_sem, local_sem):
    row, col = lax.axis_index("row"), lax.axis_index("col")
    mine = row % group
    there = row // group
    on_diagonal = there == col
    barrier = pltpu.get_barrier_semaphore()

    def partner(k):
        return (col * group + k, there)

    def copy(k):
        return pltpu.make_async_remote_copy(
            src_ref=sent.at[k],
            dst_ref=got.at[mine],
            send_sem=send_sem.at[k],
            recv_sem=recv_sem.at[mine],
            device_id=partner(k),
            device_id_type=pl.DeviceIdType.MESH,
        )

    def arrival(k):
        return pltpu.make_async_remote_copy(
            src_ref=sent.at[k],
            dst_ref=got.at[k],
            send_sem=send_sem.at[k],
            recv_sem=recv_sem.at[k],
            device_id=partner(k),
            device_id_type=pl.DeviceIdType.MESH,
        )

    order = [(mine + d) % group for d in range(group)]
    for k in order[1:]:
        pl.semaphore_signal(barrier, inc=1, device_id=partner(k), device_id_type=pl.DeviceIdType.MESH)

    @pl.when(jnp.logical_not(on_diagonal))
    def _():
        pl.semaphore_signal(barrier, inc=1, device_id=partner(mine), device_id_type=pl.DeviceIdType.MESH)

    pl.semaphore_wait(barrier, jnp.where(on_diagonal, group - 1, group))

    @pl.when(jnp.logical_not(on_diagonal))
    def _():
        copy(mine).start()

    for k in order[1:]:
        copy(k).start()

    @pl.when(on_diagonal)
    def _():
        own = pltpu.make_async_copy(sent.at[mine], got.at[mine], local_sem)
        own.start()
        own.wait()

    @pl.when(jnp.logical_not(on_diagonal))
    def _():
        arrival(mine).wait_recv()
        copy(mine).wait_send()

    for k in order[1:]:
        arrival(k).wait_recv()
        copy(k).wait_send()


def average_kernel(tile_rows, tile_cols, got, f2_ref, out_ref):
    per = LANES // tile_rows
    lane = lax.broadcasted_iota(jnp.int32, (tile_rows, LANES), 1) // tile_rows
    for g in range(got.shape[2] // LANES):
        for h in range(tile_cols // LANES):
            parts = [
                got[per * h + k, :, g * LANES : (g + 1) * LANES].astype(F32) for k in range(per)
            ]
            for cc in range(per):
                value = None
                for k in range(per):
                    shift = (tile_rows * (k - cc)) % LANES
                    moved = pltpu.roll(parts[k], shift, 1) if shift else parts[k]
                    value = moved if value is None else jnp.where(lane == k, moved, value)
                c = g * per + cc
                at = (slice(c * tile_rows, (c + 1) * tile_rows), slice(h * LANES, (h + 1) * LANES))
                out_ref[at] = (0.5 * (f2_ref[at].astype(F32) + value)).astype(BF16)


def on_device(contact_map, dilations, conv_weight, conv_gain, conv_shift, out_weight):
    channels, tile_rows, tile_cols = contact_map.shape
    blocks, _, hid, _ = conv_weight.shape
    group = tile_cols // tile_rows
    wide = tile_cols + LANES
    deep_rows, mid_rows = tile_rows + 4 * DMAX, tile_rows + 2 * DMAX
    w = (
        conv_weight.reshape(blocks, 3, 3, hid, channels)
        .transpose(0, 2, 3, 1, 4)
        .reshape(blocks, 3 * hid, 3 * channels)
    )
    gain = conv_gain[:, :, None]
    shift = conv_shift[:, :, None]
    params = pltpu.CompilerParams(vmem_limit_bytes=60000 * 1024)
    pixels = tile_rows * channels

    deep = col_rim(row_rim(contact_map, 2 * DMAX), 2 * DMAX).reshape(channels * deep_rows, wide)
    second, turned = pl.pallas_call(
        functools.partial(first_kernel, tile_rows, tile_cols),
        out_shape=(
            jax.ShapeDtypeStruct((pixels, tile_cols), BF16),
            jax.ShapeDtypeStruct((tile_cols, pixels), BF16),
        ),
        in_specs=[SMEM_SPEC] + [VMEM_SPEC] * 5,
        out_specs=(VMEM_SPEC, VMEM_SPEC),
        scratch_shapes=[
            pltpu.VMEM((wide // LANES, channels * deep_rows, LANES), F32),
            pltpu.VMEM((deep_rows, channels, wide), BF16),
            pltpu.VMEM((mid_rows, channels, wide), BF16),
            pltpu.VMEM((tile_cols // LANES, pixels, LANES), F32),
        ],
        compiler_params=params,
        name="first_blocks",
    )(dilations, deep, w, gain, shift, out_weight)

    got = pl.pallas_call(
        functools.partial(exchange_kernel, group),
        out_shape=jax.ShapeDtypeStruct((group, tile_rows, pixels), BF16),
        in_specs=[VMEM_SPEC],
        out_specs=VMEM_SPEC,
        scratch_shapes=[
            pltpu.SemaphoreType.DMA((group,)),
            pltpu.SemaphoreType.DMA((group,)),
            pltpu.SemaphoreType.DMA,
        ],
        compiler_params=pltpu.CompilerParams(collective_id=0, has_side_effects=True),
        name="exchange",
    )(turned.reshape(group, tile_rows, pixels))

    averaged = pl.pallas_call(
        functools.partial(average_kernel, tile_rows, tile_cols),
        out_shape=jax.ShapeDtypeStruct((pixels, tile_cols), BF16),
        in_specs=[VMEM_SPEC, VMEM_SPEC],
        out_specs=VMEM_SPEC,
        name="average",
    )(got, second)

    rim = col_rim(row_rim(averaged.reshape(channels, tile_rows, tile_cols), DMAX), DMAX)
    out = pl.pallas_call(
        functools.partial(last_kernel, tile_rows, tile_cols),
        out_shape=jax.ShapeDtypeStruct((pixels, tile_cols), BF16),
        in_specs=[SMEM_SPEC] + [VMEM_SPEC] * 5,
        out_specs=VMEM_SPEC,
        scratch_shapes=[
            pltpu.VMEM((wide // LANES, channels * mid_rows, LANES), F32),
            pltpu.VMEM((mid_rows, channels, wide), BF16),
            pltpu.VMEM((tile_cols // LANES, pixels, LANES), F32),
        ],
        compiler_params=params,
        name="last_block",
    )(dilations, rim.reshape(channels * mid_rows, wide), w, gain, shift, out_weight)
    return out.reshape(channels, tile_rows, tile_cols)


def solution(mesh):
    return jax.shard_map(
        on_device,
        mesh=mesh,
        in_specs=(P(None, "row", "col"), P(), P(), P(), P(), P()),
        out_specs=P(None, "row", "col"),
        check_vma=False,
    )
```

```python
import functools

import jax
import jax.numpy as jnp
from jax import lax
from jax.experimental import pallas as pl
from jax.experimental.pallas import tpu as pltpu
from jax.sharding import PartitionSpec as P

DMAX = 8
LANES = 128
F32 = jnp.float32
BF16 = jnp.bfloat16
VMEM_SPEC = pl.BlockSpec(memory_space=pltpu.VMEM)
SMEM_SPEC = pl.BlockSpec(memory_space=pltpu.SMEM)


def pack_sides(x_ref, packs_ref, tile_rows, width):
    per = LANES // width
    last = x_ref.shape[1] - LANES
    lane = lax.broadcasted_iota(jnp.int32, (tile_rows, LANES), 1)

    @pl.loop(0, packs_ref.shape[1])
    def _(g):
        left = right = None
        for j in range(per):
            start = pl.multiple_of((g * per + j) * tile_rows, tile_rows)
            rows = pl.ds(start, tile_rows)
            first = pltpu.roll(x_ref[rows, :LANES].astype(F32), width * j, 1) if j else x_ref[rows, :LANES].astype(F32)
            final = pltpu.roll(
                x_ref[rows, last:].astype(F32), (width * (j + 1)) % LANES, 1
            ) if (width * (j + 1)) % LANES else x_ref[rows, last:].astype(F32)
            here = lane >= width * j
            left = first if left is None else jnp.where(here, first, left)
            right = final if right is None else jnp.where(here, final, right)
        packs_ref[0, g] = left.astype(BF16)
        packs_ref[1, g] = right.astype(BF16)


def pack_kernel(tile_rows, width, x_ref, packs_ref):
    pack_sides(x_ref, packs_ref, tile_rows, width)


DIRECTIONS = [(1, 0), (-1, 0), (0, 1), (0, -1), (1, 1), (1, -1), (-1, 1), (-1, -1)]


def rim_kernel(width, x, packs, vert, side, corner, send_sem, recv_sem):
    rows = x.shape[1]
    here = (lax.axis_index("row"), lax.axis_index("col"))
    counts = (lax.axis_size("row"), lax.axis_size("col"))
    barrier = pltpu.get_barrier_semaphore()

    def exists(step):
        ok = None
        for at, count, d in zip(here, counts, step):
            if d:
                one = at < count - 1 if d > 0 else at > 0
                ok = one if ok is None else jnp.logical_and(ok, one)
        return ok

    def copy(n):
        dr, dc = DIRECTIONS[n]
        edge = pl.ds(rows - width, width) if dr > 0 else pl.ds(0, width)
        tall, broad = (0 if dr > 0 else 1), (0 if dc > 0 else 1)
        if dc == 0:
            src, dst = x.at[:, edge, :], vert.at[tall]
        elif dr == 0:
            src, dst = packs.at[1 - broad], side.at[broad]
        else:
            src, dst = packs.at[1 - broad, :, edge, :], corner.at[tall, broad]
        return pltpu.make_async_remote_copy(
            src_ref=src,
            dst_ref=dst,
            send_sem=send_sem.at[n],
            recv_sem=recv_sem.at[n],
            device_id=(here[0] + dr, here[1] + dc),
            device_id_type=pl.DeviceIdType.MESH,
        )

    total = jnp.int32(0)
    for step in DIRECTIONS:
        near = exists(step)
        total = total + jnp.where(near, 1, 0)

        @pl.when(near)
        def _():
            pl.semaphore_signal(
                barrier,
                inc=1,
                device_id=(here[0] + step[0], here[1] + step[1]),
                device_id_type=pl.DeviceIdType.MESH,
            )

    pl.semaphore_wait(barrier, total)
    for n, step in enumerate(DIRECTIONS):
        @pl.when(exists(step))
        def _():
            copy(n).start()

    for n, step in enumerate(DIRECTIONS):
        @pl.when(exists((-step[0], -step[1])))
        def _():
            copy(n).wait_recv()

        @pl.when(exists(step))
        def _():
            copy(n).wait_send()


def rim_of(x, packs, width, collective_id):
    channels, rows, cols = x.shape
    groups = packs.shape[1]
    anywhere = pl.BlockSpec(memory_space=pl.ANY)
    return pl.pallas_call(
        functools.partial(rim_kernel, width),
        out_shape=(
            jax.ShapeDtypeStruct((2, channels, width, cols), BF16),
            jax.ShapeDtypeStruct((2, groups, rows, LANES), BF16),
            jax.ShapeDtypeStruct((2, 2, groups, width, LANES), BF16),
        ),
        in_specs=[anywhere] * 2,
        out_specs=(anywhere,) * 3,
        scratch_shapes=[pltpu.SemaphoreType.DMA((8,)), pltpu.SemaphoreType.DMA((8,))],
        compiler_params=pltpu.CompilerParams(collective_id=collective_id, has_side_effects=True),
        name="rim_%d" % width,
    )(x, packs)


def conv_row(src_ref, i, s, w, gain, shift, expand):
    zero = jnp.zeros((), BF16)
    width = src_ref.shape[2]
    hid = gain.shape[0]
    center = src_ref[i + DMAX]
    stacked = jnp.concatenate(
        [src_ref[i + DMAX - s], center, src_ref[i + DMAX + s]], axis=0
    )
    taps = jnp.dot(w, jnp.maximum(stacked, zero), preferred_element_type=F32)
    conv = (
        pltpu.roll(taps[:hid], s, 1)
        + taps[hid : 2 * hid]
        + pltpu.roll(taps[2 * hid :], width - s, 1)
    )
    hidden = jnp.maximum(gain * conv + shift, 0.0).astype(BF16)
    return center.astype(F32) + jnp.dot(expand, hidden, preferred_element_type=F32)


def spread(x_ref, vert, side, corner, wide, by_row, rows, width):
    channels = x_ref.shape[0] // rows
    pitch = rows + 2 * width
    per = LANES // width
    row, col = lax.axis_index("row"), lax.axis_index("col")
    has_up, has_down = row > 0, row < lax.axis_size("row") - 1
    has_left, has_right = col > 0, col < lax.axis_size("col") - 1
    groups = wide.shape[0] - 1

    def filled(height, left, right, j, keep):
        lane = lax.broadcasted_iota(jnp.int32, (height, LANES), 1)
        to_right = (-(j * width)) % LANES
        to_left = (LANES - width - j * width) % LANES
        right = pltpu.roll(right, to_right, 1) if to_right else right
        left = pltpu.roll(left, to_left, 1) if to_left else left
        below = jnp.where(has_right & keep, width, 0)
        above = jnp.where(has_left & keep, LANES - width, LANES)
        return jnp.where(lane < below, right, jnp.where(lane >= above, left, 0.0))

    def kept(value, keep):
        lane = lax.broadcasted_iota(jnp.int32, value.shape, 1)
        return jnp.where(lane < jnp.where(keep, LANES, 0), value, 0.0)

    @pl.loop(0, side.shape[1])
    def _(g):
        for j in range(per):
            c = g * per + j
            start = pl.multiple_of(c * pitch, 8)
            top = pl.ds(start, width)
            middle = pl.ds(pl.multiple_of(start + width, 8), rows)
            bottom = pl.ds(pl.multiple_of(start + width + rows, 8), width)
            inside = pl.ds(pl.multiple_of(c * rows, rows), rows)
            for m in range(groups):
                lanes = slice(m * LANES, (m + 1) * LANES)
                wide[m, middle, :] = x_ref[inside, lanes].astype(F32)
                wide[m, top, :] = kept(vert[0, c, :, lanes].astype(F32), has_up)
                wide[m, bottom, :] = kept(vert[1, c, :, lanes].astype(F32), has_down)
            always = row >= 0
            wide[groups, middle, :] = filled(
                rows, side[0, g].astype(F32), side[1, g].astype(F32), j, always
            )
            wide[groups, top, :] = filled(
                width, corner[0, 0, g].astype(F32), corner[0, 1, g].astype(F32), j, has_up
            )
            wide[groups, bottom, :] = filled(
                width, corner[1, 0, g].astype(F32), corner[1, 1, g].astype(F32), j, has_down
            )

    @pl.loop(0, pitch)
    def _(i):
        for g in range(groups + 1):
            by_row[i, :, g * LANES : (g + 1) * LANES] = wide[
                g, pl.ds(i, channels, stride=pitch), :
            ].astype(BF16)


def upright(ref, k):
    hid = ref.shape[1]
    across = jnp.broadcast_to(ref[k : k + 1, :], (hid, hid))
    same = lax.broadcasted_iota(jnp.int32, (hid, hid), 0) == lax.broadcasted_iota(jnp.int32, (hid, hid), 1)
    return jnp.sum(jnp.where(same, across, 0.0), axis=1, keepdims=True)


def stack_weights(w_ref, k, stacked):
    hid, channels = w_ref.shape[2:]
    for p in range(3):
        for q in range(3):
            stacked[q * hid : (q + 1) * hid, p * channels : (p + 1) * channels] = w_ref[k, 3 * p + q]


def first_kernel(
    tile_rows, tile_cols, dil, x_ref, vert, side, corner, w_ref, gain_ref, shift_ref, expand_ref,
    f2_ref, turned_ref, wide, by_row, first, second, taps
):
    mid_rows = tile_rows + 2 * DMAX
    width = by_row.shape[2]
    channels = expand_ref.shape[1]
    spread(x_ref, vert, side, corner, wide, by_row, tile_rows, 2 * DMAX)
    row_base = lax.axis_index("row") * tile_rows - DMAX
    total_rows = lax.axis_size("row") * tile_rows
    lane = lax.broadcasted_iota(jnp.int32, (channels, width), 1)
    col = lax.axis_index("col") * tile_cols + jnp.where(lane < tile_cols + LANES // 2, lane, lane - width)
    col_inside = (col >= 0) & (col < lax.axis_size("col") * tile_cols)
    col_mask = jnp.where(col_inside, 1.0, 0.0).astype(F32)

    s0 = dil[0]
    stack_weights(w_ref, 0, taps.at[0])
    stack_weights(w_ref, 1, taps.at[1])
    gain0, shift0 = upright(gain_ref, 0), upright(shift_ref, 0)
    gain1, shift1 = upright(gain_ref, 1), upright(shift_ref, 1)

    @pl.loop(0, mid_rows, unroll=2)
    def _(i):
        value = conv_row(by_row, i, s0, taps[0], gain0, shift0, expand_ref[0])
        row = row_base + i
        inside = jnp.where((row >= 0) & (row < total_rows), 1.0, 0.0).astype(F32)
        first[i] = (value * (col_mask * inside)).astype(BF16)

    s1 = dil[1]

    @pl.loop(0, tile_rows, unroll=2)
    def _(i):
        value = conv_row(first, i, s1, taps[1], gain1, shift1, expand_ref[1])
        for g in range(second.shape[0]):
            second[g, pl.ds(i, channels, stride=tile_rows), :] = value[
                :, g * LANES : (g + 1) * LANES
            ]

    for chunk in range(channels * tile_rows // LANES):
        at = slice(chunk * LANES, (chunk + 1) * LANES)
        for g in range(second.shape[0]):
            across = slice(g * LANES, (g + 1) * LANES)
            block = second[g, at, :]
            f2_ref[at, across] = block.astype(BF16)
            turned_ref[across, at] = block.T.astype(BF16)


def last_kernel(
    tile_rows, tile_cols, dil, x_ref, vert, side, corner, w_ref, gain_ref, shift_ref, expand_ref,
    out_ref, wide, by_row, second, taps
):
    channels = expand_ref.shape[1]
    spread(x_ref, vert, side, corner, wide, by_row, tile_rows, DMAX)
    s = dil[2]
    stack_weights(w_ref, 2, taps.at[0])
    gain, shift = upright(gain_ref, 2), upright(shift_ref, 2)

    @pl.loop(0, tile_rows, unroll=2)
    def _(i):
        value = conv_row(by_row, i, s, taps[0], gain, shift, expand_ref[2])
        for g in range(second.shape[0]):
            second[g, pl.ds(i, channels, stride=tile_rows), :] = value[
                :, g * LANES : (g + 1) * LANES
            ]

    for g in range(second.shape[0]):
        out_ref[:, g * LANES : (g + 1) * LANES] = second[g].astype(BF16)


def exchange_kernel(group, sent, got, send_sem, recv_sem, local_sem):
    row, col = lax.axis_index("row"), lax.axis_index("col")
    mine = row % group
    there = row // group
    on_diagonal = there == col
    barrier = pltpu.get_barrier_semaphore()

    def partner(k):
        return (col * group + k, there)

    def copy(k):
        return pltpu.make_async_remote_copy(
            src_ref=sent.at[k],
            dst_ref=got.at[mine],
            send_sem=send_sem.at[k],
            recv_sem=recv_sem.at[mine],
            device_id=partner(k),
            device_id_type=pl.DeviceIdType.MESH,
        )

    def arrival(k):
        return pltpu.make_async_remote_copy(
            src_ref=sent.at[k],
            dst_ref=got.at[k],
            send_sem=send_sem.at[k],
            recv_sem=recv_sem.at[k],
            device_id=partner(k),
            device_id_type=pl.DeviceIdType.MESH,
        )

    order = [(mine + d) % group for d in range(group)]
    for k in order[1:]:
        pl.semaphore_signal(barrier, inc=1, device_id=partner(k), device_id_type=pl.DeviceIdType.MESH)

    @pl.when(jnp.logical_not(on_diagonal))
    def _():
        pl.semaphore_signal(barrier, inc=1, device_id=partner(mine), device_id_type=pl.DeviceIdType.MESH)

    pl.semaphore_wait(barrier, jnp.where(on_diagonal, group - 1, group))

    @pl.when(jnp.logical_not(on_diagonal))
    def _():
        copy(mine).start()

    for k in order[1:]:
        copy(k).start()

    @pl.when(on_diagonal)
    def _():
        own = pltpu.make_async_copy(sent.at[mine], got.at[mine], local_sem)
        own.start()
        own.wait()

    @pl.when(jnp.logical_not(on_diagonal))
    def _():
        arrival(mine).wait_recv()
        copy(mine).wait_send()

    for k in order[1:]:
        arrival(k).wait_recv()
        copy(k).wait_send()


def average_kernel(tile_rows, tile_cols, got, f2_ref, out_ref, packs_ref):
    per = LANES // tile_rows
    lane = lax.broadcasted_iota(jnp.int32, (tile_rows, LANES), 1) // tile_rows
    for g in range(got.shape[2] // LANES):
        for h in range(tile_cols // LANES):
            parts = [
                got[per * h + k, :, g * LANES : (g + 1) * LANES].astype(F32) for k in range(per)
            ]
            for cc in range(per):
                value = None
                for k in range(per):
                    shift = (tile_rows * (k - cc)) % LANES
                    moved = pltpu.roll(parts[k], shift, 1) if shift else parts[k]
                    value = moved if value is None else jnp.where(lane == k, moved, value)
                c = g * per + cc
                at = (slice(c * tile_rows, (c + 1) * tile_rows), slice(h * LANES, (h + 1) * LANES))
                out_ref[at] = (0.5 * (f2_ref[at].astype(F32) + value)).astype(BF16)

    pack_sides(out_ref, packs_ref, tile_rows, DMAX)


def on_device(contact_map, dilations, conv_weight, conv_gain, conv_shift, out_weight):
    channels, tile_rows, tile_cols = contact_map.shape
    blocks, _, hid, _ = conv_weight.shape
    group = tile_cols // tile_rows
    wide = tile_cols + LANES
    deep_rows, mid_rows = tile_rows + 4 * DMAX, tile_rows + 2 * DMAX
    params = pltpu.CompilerParams(vmem_limit_bytes=60000 * 1024)
    pixels = tile_rows * channels

    flat = contact_map.reshape(pixels, tile_cols)
    packs = pl.pallas_call(
        functools.partial(pack_kernel, tile_rows, 2 * DMAX),
        out_shape=jax.ShapeDtypeStruct((2, channels * 2 * DMAX // LANES, tile_rows, LANES), BF16),
        in_specs=[VMEM_SPEC],
        out_specs=VMEM_SPEC,
        name="pack",
    )(flat)
    deep = rim_of(contact_map, packs, 2 * DMAX, 1)
    second, turned = pl.pallas_call(
        functools.partial(first_kernel, tile_rows, tile_cols),
        out_shape=(
            jax.ShapeDtypeStruct((pixels, tile_cols), BF16),
            jax.ShapeDtypeStruct((tile_cols, pixels), BF16),
        ),
        in_specs=[SMEM_SPEC] + [VMEM_SPEC] * 8,
        out_specs=(VMEM_SPEC, VMEM_SPEC),
        scratch_shapes=[
            pltpu.VMEM((wide // LANES, channels * deep_rows, LANES), F32),
            pltpu.VMEM((deep_rows, channels, wide), BF16),
            pltpu.VMEM((mid_rows, channels, wide), BF16),
            pltpu.VMEM((tile_cols // LANES, pixels, LANES), F32),
            pltpu.VMEM((2, 3 * hid, 3 * channels), BF16),
        ],
        compiler_params=params,
        name="first_blocks",
    )(dilations, flat, *deep, conv_weight, conv_gain, conv_shift, out_weight)

    got = pl.pallas_call(
        functools.partial(exchange_kernel, group),
        out_shape=jax.ShapeDtypeStruct((group, tile_rows, pixels), BF16),
        in_specs=[VMEM_SPEC],
        out_specs=VMEM_SPEC,
        scratch_shapes=[
            pltpu.SemaphoreType.DMA((group,)),
            pltpu.SemaphoreType.DMA((group,)),
            pltpu.SemaphoreType.DMA,
        ],
        compiler_params=pltpu.CompilerParams(collective_id=0, has_side_effects=True),
        name="exchange",
    )(turned.reshape(group, tile_rows, pixels))

    averaged, packs = pl.pallas_call(
        functools.partial(average_kernel, tile_rows, tile_cols),
        out_shape=(
            jax.ShapeDtypeStruct((pixels, tile_cols), BF16),
            jax.ShapeDtypeStruct((2, channels * DMAX // LANES, tile_rows, LANES), BF16),
        ),
        in_specs=[VMEM_SPEC, VMEM_SPEC],
        out_specs=(VMEM_SPEC, VMEM_SPEC),
        name="average",
    )(got, second)
    rim = rim_of(averaged.reshape(channels, tile_rows, tile_cols), packs, DMAX, 2)

    out = pl.pallas_call(
        functools.partial(last_kernel, tile_rows, tile_cols),
        out_shape=jax.ShapeDtypeStruct((pixels, tile_cols), BF16),
        in_specs=[SMEM_SPEC] + [VMEM_SPEC] * 8,
        out_specs=VMEM_SPEC,
        scratch_shapes=[
            pltpu.VMEM((wide // LANES, channels * mid_rows, LANES), F32),
            pltpu.VMEM((mid_rows, channels, wide), BF16),
            pltpu.VMEM((tile_cols // LANES, pixels, LANES), F32),
            pltpu.VMEM((1, 3 * hid, 3 * channels), BF16),
        ],
        compiler_params=params,
        name="last_block",
    )(dilations, averaged, *rim, conv_weight, conv_gain, conv_shift, out_weight)
    return out.reshape(channels, tile_rows, tile_cols)


def solution(mesh):
    return jax.shard_map(
        on_device,
        mesh=mesh,
        in_specs=(P(None, "row", "col"), P(), P(), P(), P(), P()),
        out_specs=P(None, "row", "col"),
        check_vma=False,
    )
```

```python
import functools

import jax
import jax.numpy as jnp
from jax import lax
from jax.experimental import pallas as pl
from jax.experimental.pallas import tpu as pltpu
from jax.sharding import PartitionSpec as P

DMAX = 8
LANES = 128
ROWS = 4
F32 = jnp.float32
BF16 = jnp.bfloat16
VMEM_SPEC = pl.BlockSpec(memory_space=pltpu.VMEM)
SMEM_SPEC = pl.BlockSpec(memory_space=pltpu.SMEM)


def pack_sides(x_ref, packs_ref, tile_rows, width):
    per = LANES // width
    last = x_ref.shape[1] - LANES
    lane = lax.broadcasted_iota(jnp.int32, (tile_rows, LANES), 1)

    @pl.loop(0, packs_ref.shape[1])
    def _(g):
        left = right = None
        for j in range(per):
            start = pl.multiple_of((g * per + j) * tile_rows, tile_rows)
            rows = pl.ds(start, tile_rows)
            first = pltpu.roll(x_ref[rows, :LANES].astype(F32), width * j, 1) if j else x_ref[rows, :LANES].astype(F32)
            final = pltpu.roll(
                x_ref[rows, last:].astype(F32), (width * (j + 1)) % LANES, 1
            ) if (width * (j + 1)) % LANES else x_ref[rows, last:].astype(F32)
            here = lane >= width * j
            left = first if left is None else jnp.where(here, first, left)
            right = final if right is None else jnp.where(here, final, right)
        packs_ref[0, g] = left.astype(BF16)
        packs_ref[1, g] = right.astype(BF16)


def pack_kernel(tile_rows, width, x_ref, packs_ref):
    pack_sides(x_ref, packs_ref, tile_rows, width)


DIRECTIONS = [(1, 0), (-1, 0), (0, 1), (0, -1), (1, 1), (1, -1), (-1, 1), (-1, -1)]


def rim_kernel(width, x, packs, vert, side, corner, send_sem, recv_sem):
    rows = x.shape[1]
    here = (lax.axis_index("row"), lax.axis_index("col"))
    counts = (lax.axis_size("row"), lax.axis_size("col"))
    barrier = pltpu.get_barrier_semaphore()

    def exists(step):
        ok = None
        for at, count, d in zip(here, counts, step):
            if d:
                one = at < count - 1 if d > 0 else at > 0
                ok = one if ok is None else jnp.logical_and(ok, one)
        return ok

    def copy(n):
        dr, dc = DIRECTIONS[n]
        edge = pl.ds(rows - width, width) if dr > 0 else pl.ds(0, width)
        tall, broad = (0 if dr > 0 else 1), (0 if dc > 0 else 1)
        if dc == 0:
            src, dst = x.at[:, edge, :], vert.at[tall]
        elif dr == 0:
            src, dst = packs.at[1 - broad], side.at[broad]
        else:
            src, dst = packs.at[1 - broad, :, edge, :], corner.at[tall, broad]
        return pltpu.make_async_remote_copy(
            src_ref=src,
            dst_ref=dst,
            send_sem=send_sem.at[n],
            recv_sem=recv_sem.at[n],
            device_id=(here[0] + dr, here[1] + dc),
            device_id_type=pl.DeviceIdType.MESH,
        )

    total = jnp.int32(0)
    for step in DIRECTIONS:
        near = exists(step)
        total = total + jnp.where(near, 1, 0)

        @pl.when(near)
        def _():
            pl.semaphore_signal(
                barrier,
                inc=1,
                device_id=(here[0] + step[0], here[1] + step[1]),
                device_id_type=pl.DeviceIdType.MESH,
            )

    pl.semaphore_wait(barrier, total)
    for n, step in enumerate(DIRECTIONS):
        @pl.when(exists(step))
        def _():
            copy(n).start()

    for n, step in enumerate(DIRECTIONS):
        @pl.when(exists((-step[0], -step[1])))
        def _():
            copy(n).wait_recv()

        @pl.when(exists(step))
        def _():
            copy(n).wait_send()


def rim_of(x, packs, width, collective_id):
    channels, rows, cols = x.shape
    groups = packs.shape[1]
    anywhere = pl.BlockSpec(memory_space=pl.ANY)
    return pl.pallas_call(
        functools.partial(rim_kernel, width),
        out_shape=(
            jax.ShapeDtypeStruct((2, channels, width, cols), BF16),
            jax.ShapeDtypeStruct((2, groups, rows, LANES), BF16),
            jax.ShapeDtypeStruct((2, 2, groups, width, LANES), BF16),
        ),
        in_specs=[anywhere] * 2,
        out_specs=(anywhere,) * 3,
        scratch_shapes=[pltpu.SemaphoreType.DMA((8,)), pltpu.SemaphoreType.DMA((8,))],
        compiler_params=pltpu.CompilerParams(collective_id=collective_id, has_side_effects=True),
        name="rim_%d" % width,
    )(x, packs)


def conv_rows(src_ref, i, count, groups_out, s, w, gain, shift, expand):
    zero = jnp.zeros((), BF16)
    width = src_ref.shape[2]
    groups = width // LANES
    hid = gain.shape[0]
    centers = [src_ref[i + r + DMAX] for r in range(count)]
    stacked = jnp.concatenate(
        [
            jnp.concatenate([src_ref[i + r + DMAX - s], centers[r], src_ref[i + r + DMAX + s]], axis=0)
            for r in range(count)
        ],
        axis=1,
    )
    taps = jnp.dot(w, jnp.maximum(stacked, zero), preferred_element_type=F32)
    lane = lax.broadcasted_iota(jnp.int32, (hid, LANES), 1)
    from_left, from_right = lane >= s, lane < LANES - s
    hidden = []
    for r in range(count):
        piece = [taps[:, r * width + m * LANES : r * width + (m + 1) * LANES] for m in range(groups)]
        low = [pltpu.roll(y[:hid], s, 1) for y in piece]
        high = [pltpu.roll(y[2 * hid :], LANES - s, 1) for y in piece]
        for m in range(groups_out):
            conv = (
                jnp.where(from_left, low[m], low[m - 1])
                + piece[m][hid : 2 * hid]
                + jnp.where(from_right, high[m], high[(m + 1) % groups])
            )
            hidden.append(jnp.maximum(gain * conv + shift, 0.0).astype(BF16))
    added = jnp.dot(expand, jnp.concatenate(hidden, axis=1), preferred_element_type=F32)
    return [
        [
            centers[r][:, m * LANES : (m + 1) * LANES].astype(F32)
            + added[:, (r * groups_out + m) * LANES : (r * groups_out + m + 1) * LANES]
            for m in range(groups_out)
        ]
        for r in range(count)
    ]


def spread(x_ref, vert, side, corner, wide, by_row, rows, width):
    channels = x_ref.shape[0] // rows
    pitch = rows + 2 * width
    per = LANES // width
    row, col = lax.axis_index("row"), lax.axis_index("col")
    has_up, has_down = row > 0, row < lax.axis_size("row") - 1
    has_left, has_right = col > 0, col < lax.axis_size("col") - 1
    groups = wide.shape[0] - 1

    def filled(height, left, right, j, keep):
        lane = lax.broadcasted_iota(jnp.int32, (height, LANES), 1)
        to_right = (-(j * width)) % LANES
        to_left = (LANES - width - j * width) % LANES
        right = pltpu.roll(right, to_right, 1) if to_right else right
        left = pltpu.roll(left, to_left, 1) if to_left else left
        below = jnp.where(has_right & keep, width, 0)
        above = jnp.where(has_left & keep, LANES - width, LANES)
        return jnp.where(lane < below, right, jnp.where(lane >= above, left, 0.0))

    def kept(value, keep):
        lane = lax.broadcasted_iota(jnp.int32, value.shape, 1)
        return jnp.where(lane < jnp.where(keep, LANES, 0), value, 0.0)

    @pl.loop(0, side.shape[1])
    def _(g):
        for j in range(per):
            c = g * per + j
            start = pl.multiple_of(c * pitch, 8)
            top = pl.ds(start, width)
            middle = pl.ds(pl.multiple_of(start + width, 8), rows)
            bottom = pl.ds(pl.multiple_of(start + width + rows, 8), width)
            inside = pl.ds(pl.multiple_of(c * rows, rows), rows)
            for m in range(groups):
                lanes = slice(m * LANES, (m + 1) * LANES)
                wide[m, middle, :] = x_ref[inside, lanes].astype(F32)
                wide[m, top, :] = kept(vert[0, c, :, lanes].astype(F32), has_up)
                wide[m, bottom, :] = kept(vert[1, c, :, lanes].astype(F32), has_down)
            always = row >= 0
            wide[groups, middle, :] = filled(
                rows, side[0, g].astype(F32), side[1, g].astype(F32), j, always
            )
            wide[groups, top, :] = filled(
                width, corner[0, 0, g].astype(F32), corner[0, 1, g].astype(F32), j, has_up
            )
            wide[groups, bottom, :] = filled(
                width, corner[1, 0, g].astype(F32), corner[1, 1, g].astype(F32), j, has_down
            )

    @pl.loop(0, pitch)
    def _(i):
        for g in range(groups + 1):
            by_row[i, :, g * LANES : (g + 1) * LANES] = wide[
                g, pl.ds(i, channels, stride=pitch), :
            ].astype(BF16)


def upright(ref, k):
    hid = ref.shape[1]
    across = jnp.broadcast_to(ref[k : k + 1, :], (hid, hid))
    same = lax.broadcasted_iota(jnp.int32, (hid, hid), 0) == lax.broadcasted_iota(jnp.int32, (hid, hid), 1)
    return jnp.sum(jnp.where(same, across, 0.0), axis=1, keepdims=True)


def stack_weights(w_ref, k, stacked):
    hid, channels = w_ref.shape[2:]
    for p in range(3):
        for q in range(3):
            stacked[q * hid : (q + 1) * hid, p * channels : (p + 1) * channels] = w_ref[k, 3 * p + q]


def first_kernel(
    tile_rows, tile_cols, dil, x_ref, vert, side, corner, w_ref, gain_ref, shift_ref, expand_ref,
    f2_ref, turned_ref, wide, by_row, first, second, taps
):
    mid_rows = tile_rows + 2 * DMAX
    width = by_row.shape[2]
    channels = expand_ref.shape[1]
    spread(x_ref, vert, side, corner, wide, by_row, tile_rows, 2 * DMAX)
    row_base = lax.axis_index("row") * tile_rows - DMAX
    total_rows = lax.axis_size("row") * tile_rows
    lane = lax.broadcasted_iota(jnp.int32, (channels, width), 1)
    col = lax.axis_index("col") * tile_cols + jnp.where(lane < tile_cols + LANES // 2, lane, lane - width)
    col_inside = (col >= 0) & (col < lax.axis_size("col") * tile_cols)
    col_mask = jnp.where(col_inside, 1.0, 0.0).astype(F32)

    s0 = dil[0]
    stack_weights(w_ref, 0, taps.at[0])
    stack_weights(w_ref, 1, taps.at[1])
    gain0, shift0 = upright(gain_ref, 0), upright(shift_ref, 0)
    gain1, shift1 = upright(gain_ref, 1), upright(shift_ref, 1)

    @pl.loop(0, mid_rows, step=ROWS)
    def _(i):
        rows = conv_rows(by_row, i, ROWS, width // LANES, s0, taps[0], gain0, shift0, expand_ref[0])
        for r, pieces in enumerate(rows):
            row = row_base + i + r
            inside = jnp.where((row >= 0) & (row < total_rows), 1.0, 0.0).astype(F32)
            for m, value in enumerate(pieces):
                lanes = slice(m * LANES, (m + 1) * LANES)
                first[i + r, :, lanes] = (value * (col_mask[:, lanes] * inside)).astype(BF16)

    s1 = dil[1]

    @pl.loop(0, tile_rows, step=ROWS)
    def _(i):
        rows = conv_rows(first, i, ROWS, tile_cols // LANES, s1, taps[1], gain1, shift1, expand_ref[1])
        for r, pieces in enumerate(rows):
            for m, value in enumerate(pieces):
                second[m, pl.ds(i + r, channels, stride=tile_rows), :] = value

    for chunk in range(channels * tile_rows // LANES):
        at = slice(chunk * LANES, (chunk + 1) * LANES)
        for g in range(second.shape[0]):
            across = slice(g * LANES, (g + 1) * LANES)
            block = second[g, at, :]
            f2_ref[at, across] = block.astype(BF16)
            turned_ref[across, at] = block.T.astype(BF16)


def last_kernel(
    tile_rows, tile_cols, dil, x_ref, vert, side, corner, w_ref, gain_ref, shift_ref, expand_ref,
    out_ref, wide, by_row, second, taps
):
    channels = expand_ref.shape[1]
    spread(x_ref, vert, side, corner, wide, by_row, tile_rows, DMAX)
    s = dil[2]
    stack_weights(w_ref, 2, taps.at[0])
    gain, shift = upright(gain_ref, 2), upright(shift_ref, 2)

    @pl.loop(0, tile_rows, step=ROWS)
    def _(i):
        rows = conv_rows(by_row, i, ROWS, tile_cols // LANES, s, taps[0], gain, shift, expand_ref[2])
        for r, pieces in enumerate(rows):
            for m, value in enumerate(pieces):
                second[m, pl.ds(i + r, channels, stride=tile_rows), :] = value

    for g in range(second.shape[0]):
        out_ref[:, g * LANES : (g + 1) * LANES] = second[g].astype(BF16)


def exchange_kernel(group, sent, got, send_sem, recv_sem, local_sem):
    row, col = lax.axis_index("row"), lax.axis_index("col")
    mine = row % group
    there = row // group
    on_diagonal = there == col
    barrier = pltpu.get_barrier_semaphore()

    def partner(k):
        return (col * group + k, there)

    def copy(k):
        return pltpu.make_async_remote_copy(
            src_ref=sent.at[k],
            dst_ref=got.at[mine],
            send_sem=send_sem.at[k],
            recv_sem=recv_sem.at[mine],
            device_id=partner(k),
            device_id_type=pl.DeviceIdType.MESH,
        )

    def arrival(k):
        return pltpu.make_async_remote_copy(
            src_ref=sent.at[k],
            dst_ref=got.at[k],
            send_sem=send_sem.at[k],
            recv_sem=recv_sem.at[k],
            device_id=partner(k),
            device_id_type=pl.DeviceIdType.MESH,
        )

    order = [(mine + d) % group for d in range(group)]
    for k in order[1:]:
        pl.semaphore_signal(barrier, inc=1, device_id=partner(k), device_id_type=pl.DeviceIdType.MESH)

    @pl.when(jnp.logical_not(on_diagonal))
    def _():
        pl.semaphore_signal(barrier, inc=1, device_id=partner(mine), device_id_type=pl.DeviceIdType.MESH)

    pl.semaphore_wait(barrier, jnp.where(on_diagonal, group - 1, group))

    @pl.when(jnp.logical_not(on_diagonal))
    def _():
        copy(mine).start()

    for k in order[1:]:
        copy(k).start()

    @pl.when(on_diagonal)
    def _():
        own = pltpu.make_async_copy(sent.at[mine], got.at[mine], local_sem)
        own.start()
        own.wait()

    @pl.when(jnp.logical_not(on_diagonal))
    def _():
        arrival(mine).wait_recv()
        copy(mine).wait_send()

    for k in order[1:]:
        arrival(k).wait_recv()
        copy(k).wait_send()


def average_kernel(tile_rows, tile_cols, got, f2_ref, out_ref, packs_ref):
    per = LANES // tile_rows
    lane = lax.broadcasted_iota(jnp.int32, (tile_rows, LANES), 1) // tile_rows
    for g in range(got.shape[2] // LANES):
        for h in range(tile_cols // LANES):
            parts = [
                got[per * h + k, :, g * LANES : (g + 1) * LANES].astype(F32) for k in range(per)
            ]
            for cc in range(per):
                value = None
                for k in range(per):
                    shift = (tile_rows * (k - cc)) % LANES
                    moved = pltpu.roll(parts[k], shift, 1) if shift else parts[k]
                    value = moved if value is None else jnp.where(lane == k, moved, value)
                c = g * per + cc
                at = (slice(c * tile_rows, (c + 1) * tile_rows), slice(h * LANES, (h + 1) * LANES))
                out_ref[at] = (0.5 * (f2_ref[at].astype(F32) + value)).astype(BF16)

    pack_sides(out_ref, packs_ref, tile_rows, DMAX)


def on_device(contact_map, dilations, conv_weight, conv_gain, conv_shift, out_weight):
    channels, tile_rows, tile_cols = contact_map.shape
    blocks, _, hid, _ = conv_weight.shape
    group = tile_cols // tile_rows
    wide = tile_cols + LANES
    deep_rows, mid_rows = tile_rows + 4 * DMAX, tile_rows + 2 * DMAX
    params = pltpu.CompilerParams(vmem_limit_bytes=60000 * 1024)
    pixels = tile_rows * channels

    flat = contact_map.reshape(pixels, tile_cols)
    packs = pl.pallas_call(
        functools.partial(pack_kernel, tile_rows, 2 * DMAX),
        out_shape=jax.ShapeDtypeStruct((2, channels * 2 * DMAX // LANES, tile_rows, LANES), BF16),
        in_specs=[VMEM_SPEC],
        out_specs=VMEM_SPEC,
        name="pack",
    )(flat)
    deep = rim_of(contact_map, packs, 2 * DMAX, 1)
    second, turned = pl.pallas_call(
        functools.partial(first_kernel, tile_rows, tile_cols),
        out_shape=(
            jax.ShapeDtypeStruct((pixels, tile_cols), BF16),
            jax.ShapeDtypeStruct((tile_cols, pixels), BF16),
        ),
        in_specs=[SMEM_SPEC] + [VMEM_SPEC] * 8,
        out_specs=(VMEM_SPEC, VMEM_SPEC),
        scratch_shapes=[
            pltpu.VMEM((wide // LANES, channels * deep_rows, LANES), F32),
            pltpu.VMEM((deep_rows, channels, wide), BF16),
            pltpu.VMEM((mid_rows, channels, wide), BF16),
            pltpu.VMEM((tile_cols // LANES, pixels, LANES), F32),
            pltpu.VMEM((2, 3 * hid, 3 * channels), BF16),
        ],
        compiler_params=params,
        name="first_blocks",
    )(dilations, flat, *deep, conv_weight, conv_gain, conv_shift, out_weight)

    got = pl.pallas_call(
        functools.partial(exchange_kernel, group),
        out_shape=jax.ShapeDtypeStruct((group, tile_rows, pixels), BF16),
        in_specs=[VMEM_SPEC],
        out_specs=VMEM_SPEC,
        scratch_shapes=[
            pltpu.SemaphoreType.DMA((group,)),
            pltpu.SemaphoreType.DMA((group,)),
            pltpu.SemaphoreType.DMA,
        ],
        compiler_params=pltpu.CompilerParams(collective_id=0, has_side_effects=True),
        name="exchange",
    )(turned.reshape(group, tile_rows, pixels))

    averaged, packs = pl.pallas_call(
        functools.partial(average_kernel, tile_rows, tile_cols),
        out_shape=(
            jax.ShapeDtypeStruct((pixels, tile_cols), BF16),
            jax.ShapeDtypeStruct((2, channels * DMAX // LANES, tile_rows, LANES), BF16),
        ),
        in_specs=[VMEM_SPEC, VMEM_SPEC],
        out_specs=(VMEM_SPEC, VMEM_SPEC),
        name="average",
    )(got, second)
    rim = rim_of(averaged.reshape(channels, tile_rows, tile_cols), packs, DMAX, 2)

    out = pl.pallas_call(
        functools.partial(last_kernel, tile_rows, tile_cols),
        out_shape=jax.ShapeDtypeStruct((pixels, tile_cols), BF16),
        in_specs=[SMEM_SPEC] + [VMEM_SPEC] * 8,
        out_specs=VMEM_SPEC,
        scratch_shapes=[
            pltpu.VMEM((wide // LANES, channels * mid_rows, LANES), F32),
            pltpu.VMEM((mid_rows, channels, wide), BF16),
            pltpu.VMEM((tile_cols // LANES, pixels, LANES), F32),
            pltpu.VMEM((1, 3 * hid, 3 * channels), BF16),
        ],
        compiler_params=params,
        name="last_block",
    )(dilations, averaged, *rim, conv_weight, conv_gain, conv_shift, out_weight)
    return out.reshape(channels, tile_rows, tile_cols)


def solution(mesh):
    return jax.shard_map(
        on_device,
        mesh=mesh,
        in_specs=(P(None, "row", "col"), P(), P(), P(), P(), P()),
        out_specs=P(None, "row", "col"),
        check_vma=False,
    )
```

```python
import functools

import jax
import jax.numpy as jnp
from jax import lax
from jax.experimental import pallas as pl
from jax.experimental.pallas import tpu as pltpu
from jax.sharding import PartitionSpec as P

DMAX = 8
LANES = 128
ROWS = 4
TURN_FIRST = True
F32 = jnp.float32
BF16 = jnp.bfloat16
VMEM_SPEC = pl.BlockSpec(memory_space=pltpu.VMEM)
SMEM_SPEC = pl.BlockSpec(memory_space=pltpu.SMEM)


def pack_sides(x_ref, packs_ref, tile_rows, width):
    per = LANES // width
    last = x_ref.shape[1] - LANES
    lane = lax.broadcasted_iota(jnp.int32, (tile_rows, LANES), 1)

    @pl.loop(0, packs_ref.shape[1])
    def _(g):
        left = right = None
        for j in range(per):
            start = pl.multiple_of((g * per + j) * tile_rows, tile_rows)
            rows = pl.ds(start, tile_rows)
            first = pltpu.roll(x_ref[rows, :LANES].astype(F32), width * j, 1) if j else x_ref[rows, :LANES].astype(F32)
            final = pltpu.roll(
                x_ref[rows, last:].astype(F32), (width * (j + 1)) % LANES, 1
            ) if (width * (j + 1)) % LANES else x_ref[rows, last:].astype(F32)
            here = lane >= width * j
            left = first if left is None else jnp.where(here, first, left)
            right = final if right is None else jnp.where(here, final, right)
        packs_ref[0, g] = left.astype(BF16)
        packs_ref[1, g] = right.astype(BF16)


def pack_kernel(tile_rows, width, x_ref, packs_ref):
    pack_sides(x_ref, packs_ref, tile_rows, width)


DIRECTIONS = [(1, 0), (-1, 0), (0, 1), (0, -1), (1, 1), (1, -1), (-1, 1), (-1, -1)]


def rim_kernel(width, x, packs, vert, side, corner, send_sem, recv_sem):
    rows = x.shape[1]
    here = (lax.axis_index("row"), lax.axis_index("col"))
    counts = (lax.axis_size("row"), lax.axis_size("col"))
    barrier = pltpu.get_barrier_semaphore()

    def exists(step):
        ok = None
        for at, count, d in zip(here, counts, step):
            if d:
                one = at < count - 1 if d > 0 else at > 0
                ok = one if ok is None else jnp.logical_and(ok, one)
        return ok

    def copy(n):
        dr, dc = DIRECTIONS[n]
        edge = pl.ds(rows - width, width) if dr > 0 else pl.ds(0, width)
        tall, broad = (0 if dr > 0 else 1), (0 if dc > 0 else 1)
        if dc == 0:
            src, dst = x.at[:, edge, :], vert.at[tall]
        elif dr == 0:
            src, dst = packs.at[1 - broad], side.at[broad]
        else:
            src, dst = packs.at[1 - broad, :, edge, :], corner.at[tall, broad]
        return pltpu.make_async_remote_copy(
            src_ref=src,
            dst_ref=dst,
            send_sem=send_sem.at[n],
            recv_sem=recv_sem.at[n],
            device_id=(here[0] + dr, here[1] + dc),
            device_id_type=pl.DeviceIdType.MESH,
        )

    total = jnp.int32(0)
    for step in DIRECTIONS:
        near = exists(step)
        total = total + jnp.where(near, 1, 0)

        @pl.when(near)
        def _():
            pl.semaphore_signal(
                barrier,
                inc=1,
                device_id=(here[0] + step[0], here[1] + step[1]),
                device_id_type=pl.DeviceIdType.MESH,
            )

    pl.semaphore_wait(barrier, total)
    for n, step in enumerate(DIRECTIONS):
        @pl.when(exists(step))
        def _():
            copy(n).start()

    for n, step in enumerate(DIRECTIONS):
        @pl.when(exists((-step[0], -step[1])))
        def _():
            copy(n).wait_recv()

        @pl.when(exists(step))
        def _():
            copy(n).wait_send()


def rim_of(x, packs, width, collective_id):
    channels, rows, cols = x.shape
    groups = packs.shape[1]
    anywhere = pl.BlockSpec(memory_space=pl.ANY)
    return pl.pallas_call(
        functools.partial(rim_kernel, width),
        out_shape=(
            jax.ShapeDtypeStruct((2, channels, width, cols), BF16),
            jax.ShapeDtypeStruct((2, groups, rows, LANES), BF16),
            jax.ShapeDtypeStruct((2, 2, groups, width, LANES), BF16),
        ),
        in_specs=[anywhere] * 2,
        out_specs=(anywhere,) * 3,
        scratch_shapes=[pltpu.SemaphoreType.DMA((8,)), pltpu.SemaphoreType.DMA((8,))],
        compiler_params=pltpu.CompilerParams(collective_id=collective_id, has_side_effects=True),
        name="rim_%d" % width,
    )(x, packs)


def conv_rows(src_ref, i, count, groups_out, s, w, gain, shift, expand):
    zero = jnp.zeros((), BF16)
    width = src_ref.shape[2]
    groups = width // LANES
    hid = gain.shape[0]
    centers = [src_ref[i + r + DMAX] for r in range(count)]
    stacked = jnp.concatenate(
        [
            jnp.concatenate([src_ref[i + r + DMAX - s], centers[r], src_ref[i + r + DMAX + s]], axis=0)
            for r in range(count)
        ],
        axis=1,
    )
    taps = jnp.dot(w, jnp.maximum(stacked, zero), preferred_element_type=F32)
    lane = lax.broadcasted_iota(jnp.int32, (hid, LANES), 1)
    from_left, from_right = lane >= s, lane < LANES - s
    hidden = []
    for r in range(count):
        piece = [taps[:, r * width + m * LANES : r * width + (m + 1) * LANES] for m in range(groups)]
        low = [pltpu.roll(y[:hid], s, 1) for y in piece]
        high = [pltpu.roll(y[2 * hid :], LANES - s, 1) for y in piece]
        for m in range(groups_out):
            conv = (
                jnp.where(from_left, low[m], low[m - 1])
                + piece[m][hid : 2 * hid]
                + jnp.where(from_right, high[m], high[(m + 1) % groups])
            )
            hidden.append(jnp.maximum(gain * conv + shift, 0.0).astype(BF16))
    added = jnp.dot(expand, jnp.concatenate(hidden, axis=1), preferred_element_type=F32)
    return [
        [
            centers[r][:, m * LANES : (m + 1) * LANES].astype(F32)
            + added[:, (r * groups_out + m) * LANES : (r * groups_out + m + 1) * LANES]
            for m in range(groups_out)
        ]
        for r in range(count)
    ]


def spread(x_ref, vert, side, corner, wide, by_row, rows, width):
    channels = x_ref.shape[0] // rows
    pitch = rows + 2 * width
    per = LANES // width
    row, col = lax.axis_index("row"), lax.axis_index("col")
    has_up, has_down = row > 0, row < lax.axis_size("row") - 1
    has_left, has_right = col > 0, col < lax.axis_size("col") - 1
    groups = wide.shape[0] - 1

    def filled(height, left, right, j, keep):
        lane = lax.broadcasted_iota(jnp.int32, (height, LANES), 1)
        to_right = (-(j * width)) % LANES
        to_left = (LANES - width - j * width) % LANES
        right = pltpu.roll(right, to_right, 1) if to_right else right
        left = pltpu.roll(left, to_left, 1) if to_left else left
        below = jnp.where(has_right & keep, width, 0)
        above = jnp.where(has_left & keep, LANES - width, LANES)
        return jnp.where(lane < below, right, jnp.where(lane >= above, left, 0.0))

    def kept(value, keep):
        lane = lax.broadcasted_iota(jnp.int32, value.shape, 1)
        return jnp.where(lane < jnp.where(keep, LANES, 0), value, 0.0)

    @pl.loop(0, side.shape[1])
    def _(g):
        for j in range(per):
            c = g * per + j
            start = pl.multiple_of(c * pitch, 8)
            top = pl.ds(start, width)
            middle = pl.ds(pl.multiple_of(start + width, 8), rows)
            bottom = pl.ds(pl.multiple_of(start + width + rows, 8), width)
            inside = pl.ds(pl.multiple_of(c * rows, rows), rows)
            for m in range(groups):
                lanes = slice(m * LANES, (m + 1) * LANES)
                wide[m, middle, :] = x_ref[inside, lanes].astype(F32)
                wide[m, top, :] = kept(vert[0, c, :, lanes].astype(F32), has_up)
                wide[m, bottom, :] = kept(vert[1, c, :, lanes].astype(F32), has_down)
            always = row >= 0
            wide[groups, middle, :] = filled(
                rows, side[0, g].astype(F32), side[1, g].astype(F32), j, always
            )
            wide[groups, top, :] = filled(
                width, corner[0, 0, g].astype(F32), corner[0, 1, g].astype(F32), j, has_up
            )
            wide[groups, bottom, :] = filled(
                width, corner[1, 0, g].astype(F32), corner[1, 1, g].astype(F32), j, has_down
            )

    @pl.loop(0, pitch)
    def _(i):
        for g in range(groups + 1):
            by_row[i, :, g * LANES : (g + 1) * LANES] = wide[
                g, pl.ds(i, channels, stride=pitch), :
            ].astype(BF16)


def upright(ref, k):
    hid = ref.shape[1]
    across = jnp.broadcast_to(ref[k : k + 1, :], (hid, hid))
    same = lax.broadcasted_iota(jnp.int32, (hid, hid), 0) == lax.broadcasted_iota(jnp.int32, (hid, hid), 1)
    return jnp.sum(jnp.where(same, across, 0.0), axis=1, keepdims=True)


def stack_weights(w_ref, k, stacked):
    hid, channels = w_ref.shape[2:]
    for p in range(3):
        for q in range(3):
            stacked[q * hid : (q + 1) * hid, p * channels : (p + 1) * channels] = w_ref[k, 3 * p + q]


def first_kernel(
    tile_rows, tile_cols, dil, x_ref, vert, side, corner, w_ref, gain_ref, shift_ref, expand_ref,
    f2_ref, turned_ref, wide, by_row, first, second, taps
):
    mid_rows = tile_rows + 2 * DMAX
    width = by_row.shape[2]
    channels = expand_ref.shape[1]
    spread(x_ref, vert, side, corner, wide, by_row, tile_rows, 2 * DMAX)
    row_base = lax.axis_index("row") * tile_rows - DMAX
    total_rows = lax.axis_size("row") * tile_rows
    lane = lax.broadcasted_iota(jnp.int32, (channels, width), 1)
    col = lax.axis_index("col") * tile_cols + jnp.where(lane < tile_cols + LANES // 2, lane, lane - width)
    col_inside = (col >= 0) & (col < lax.axis_size("col") * tile_cols)
    col_mask = jnp.where(col_inside, 1.0, 0.0).astype(F32)

    s0 = dil[0]
    stack_weights(w_ref, 0, taps.at[0])
    stack_weights(w_ref, 1, taps.at[1])
    gain0, shift0 = upright(gain_ref, 0), upright(shift_ref, 0)
    gain1, shift1 = upright(gain_ref, 1), upright(shift_ref, 1)

    @pl.loop(0, mid_rows, step=ROWS)
    def _(i):
        rows = conv_rows(by_row, i, ROWS, width // LANES, s0, taps[0], gain0, shift0, expand_ref[0])
        for r, pieces in enumerate(rows):
            row = row_base + i + r
            inside = jnp.where((row >= 0) & (row < total_rows), 1.0, 0.0).astype(F32)
            for m, value in enumerate(pieces):
                lanes = slice(m * LANES, (m + 1) * LANES)
                first[i + r, :, lanes] = (value * (col_mask[:, lanes] * inside)).astype(BF16)

    s1 = dil[1]

    @pl.loop(0, tile_rows, step=ROWS)
    def _(i):
        rows = conv_rows(first, i, ROWS, tile_cols // LANES, s1, taps[1], gain1, shift1, expand_ref[1])
        for r, pieces in enumerate(rows):
            for m, value in enumerate(pieces):
                second[m, pl.ds(i + r, channels, stride=tile_rows), :] = value

    for chunk in range(channels * tile_rows // LANES):
        at = slice(chunk * LANES, (chunk + 1) * LANES)
        for g in range(second.shape[0]):
            across = slice(g * LANES, (g + 1) * LANES)
            block = second[g, at, :]
            f2_ref[at, across] = block.astype(BF16)
            turned_ref[across, at] = block.T.astype(BF16)


def last_kernel(
    tile_rows, tile_cols, dil, x_ref, vert, side, corner, w_ref, gain_ref, shift_ref, expand_ref,
    out_ref, wide, by_row, second, taps
):
    channels = expand_ref.shape[1]
    spread(x_ref, vert, side, corner, wide, by_row, tile_rows, DMAX)
    s = dil[2]
    stack_weights(w_ref, 2, taps.at[0])
    gain, shift = upright(gain_ref, 2), upright(shift_ref, 2)

    @pl.loop(0, tile_rows, step=ROWS)
    def _(i):
        rows = conv_rows(by_row, i, ROWS, tile_cols // LANES, s, taps[0], gain, shift, expand_ref[2])
        for r, pieces in enumerate(rows):
            for m, value in enumerate(pieces):
                second[m, pl.ds(i + r, channels, stride=tile_rows), :] = value

    for g in range(second.shape[0]):
        out_ref[:, g * LANES : (g + 1) * LANES] = second[g].astype(BF16)


def exchange_kernel(group, sent, got, hold, send_sem, recv_sem, send_half, recv_half, hold_sem, pass_sem, local_sem):
    row, col = lax.axis_index("row"), lax.axis_index("col")
    cols = lax.axis_size("col")
    mine, there = row % group, row // group
    on_diagonal = there == col
    off_diagonal = jnp.logical_not(on_diagonal)
    half = sent.shape[1] // 2
    near, far = pl.ds(0, half), pl.ds(half, half)
    mesh_id = pl.DeviceIdType.MESH
    barrier = pltpu.get_barrier_semaphore()
    order = [(mine + d) % group for d in range(group)]

    def partner(k):
        return (col * group + k, there)

    def remote(src, dst, send, recv, device):
        return pltpu.make_async_remote_copy(
            src_ref=src, dst_ref=dst, send_sem=send, recv_sem=recv, device_id=device, device_id_type=mesh_id
        )

    def whole(k, slot):
        return remote(sent.at[k], got.at[slot], send_sem.at[k], recv_sem.at[slot], partner(k))

    def direct(k, slot):
        return remote(sent.at[k, near], got.at[slot, near], send_sem.at[k], recv_sem.at[slot], partner(k))

    def relayed(k):
        device, slot = ((row, there), col * group + k) if TURN_FIRST else ((col * group + k, col), row)
        return remote(sent.at[k, far], hold.at[slot], send_half.at[k], hold_sem.at[slot], device)

    def passed(q):
        device, slot = ((q, col), mine) if TURN_FIRST else ((row, q // group), q % group)
        return remote(hold.at[q], got.at[slot, far], pass_sem.at[q], recv_half.at[slot], device)

    def held(q):
        return remote(hold.at[q], hold.at[q], pass_sem.at[q], hold_sem.at[q], partner((mine + 1) % group))

    def landed(k):
        return remote(hold.at[0], got.at[k, far], send_half.at[k], recv_half.at[k], partner(k))

    def greet(device):
        pl.semaphore_signal(barrier, inc=1, device_id=device, device_id_type=mesh_id)

    through = [((col + e) % cols * group + (mine - d) % group) for d in range(group) for e in range(1, cols)]
    for k in order[1:]:
        greet(partner(k))

    @pl.when(on_diagonal)
    def _():
        for q in through:
            greet((q, col))
        for e in range(1, cols):
            greet((row, (col + e) % cols))

    @pl.when(off_diagonal)
    def _():
        greet(partner(mine))
        for k in order:
            greet((col * group + k, col))
        greet((row, there))

    pl.semaphore_wait(
        barrier, jnp.where(on_diagonal, group - 1 + (cols - 1) * (group + 1), 2 * group + 1)
    )

    @pl.when(off_diagonal)
    def _():
        for k in order:
            relayed(k).start()
            direct(k, mine).start()
        for k in order:
            direct(k, k).wait_recv()
            landed(k).wait_recv()
        for k in order:
            direct(k, mine).wait_send()
            relayed(k).wait_send()

    @pl.when(on_diagonal)
    def _():
        own = pltpu.make_async_copy(sent.at[mine], got.at[mine], local_sem)
        own.start()
        for k in order[1:]:
            whole(k, mine).start()
        for q in through:
            held(q).wait_recv()
            passed(q).start()
        for k in order[1:]:
            whole(k, k).wait_recv()
            whole(k, mine).wait_send()
        for q in through:
            passed(q).wait_send()
        own.wait()


def average_kernel(tile_rows, tile_cols, got, f2_ref, out_ref, packs_ref):
    per = LANES // tile_rows
    lane = lax.broadcasted_iota(jnp.int32, (tile_rows, LANES), 1) // tile_rows
    for g in range(got.shape[2] // LANES):
        for h in range(tile_cols // LANES):
            parts = [
                got[per * h + k, :, g * LANES : (g + 1) * LANES].astype(F32) for k in range(per)
            ]
            for cc in range(per):
                value = None
                for k in range(per):
                    shift = (tile_rows * (k - cc)) % LANES
                    moved = pltpu.roll(parts[k], shift, 1) if shift else parts[k]
                    value = moved if value is None else jnp.where(lane == k, moved, value)
                c = g * per + cc
                at = (slice(c * tile_rows, (c + 1) * tile_rows), slice(h * LANES, (h + 1) * LANES))
                out_ref[at] = (0.5 * (f2_ref[at].astype(F32) + value)).astype(BF16)

    pack_sides(out_ref, packs_ref, tile_rows, DMAX)


def on_device(contact_map, dilations, conv_weight, conv_gain, conv_shift, out_weight):
    channels, tile_rows, tile_cols = contact_map.shape
    blocks, _, hid, _ = conv_weight.shape
    group = tile_cols // tile_rows
    wide = tile_cols + LANES
    deep_rows, mid_rows = tile_rows + 4 * DMAX, tile_rows + 2 * DMAX
    params = pltpu.CompilerParams(vmem_limit_bytes=60000 * 1024)
    pixels = tile_rows * channels

    flat = contact_map.reshape(pixels, tile_cols)
    packs = pl.pallas_call(
        functools.partial(pack_kernel, tile_rows, 2 * DMAX),
        out_shape=jax.ShapeDtypeStruct((2, channels * 2 * DMAX // LANES, tile_rows, LANES), BF16),
        in_specs=[VMEM_SPEC],
        out_specs=VMEM_SPEC,
        name="pack",
    )(flat)
    deep = rim_of(contact_map, packs, 2 * DMAX, 1)
    second, turned = pl.pallas_call(
        functools.partial(first_kernel, tile_rows, tile_cols),
        out_shape=(
            jax.ShapeDtypeStruct((pixels, tile_cols), BF16),
            jax.ShapeDtypeStruct((tile_cols, pixels), BF16),
        ),
        in_specs=[SMEM_SPEC] + [VMEM_SPEC] * 8,
        out_specs=(VMEM_SPEC, VMEM_SPEC),
        scratch_shapes=[
            pltpu.VMEM((wide // LANES, channels * deep_rows, LANES), F32),
            pltpu.VMEM((deep_rows, channels, wide), BF16),
            pltpu.VMEM((mid_rows, channels, wide), BF16),
            pltpu.VMEM((tile_cols // LANES, pixels, LANES), F32),
            pltpu.VMEM((2, 3 * hid, 3 * channels), BF16),
        ],
        compiler_params=params,
        name="first_blocks",
    )(dilations, flat, *deep, conv_weight, conv_gain, conv_shift, out_weight)

    got = pl.pallas_call(
        functools.partial(exchange_kernel, group),
        out_shape=jax.ShapeDtypeStruct((group, tile_rows, pixels), BF16),
        in_specs=[VMEM_SPEC],
        out_specs=VMEM_SPEC,
        scratch_shapes=[pltpu.VMEM((lax.axis_size("row"), tile_rows // 2, pixels), BF16)]
        + [pltpu.SemaphoreType.DMA((group,))] * 4
        + [pltpu.SemaphoreType.DMA((lax.axis_size("row"),))] * 2
        + [pltpu.SemaphoreType.DMA],
        compiler_params=pltpu.CompilerParams(collective_id=0, has_side_effects=True),
        name="exchange",
    )(turned.reshape(group, tile_rows, pixels))

    averaged, packs = pl.pallas_call(
        functools.partial(average_kernel, tile_rows, tile_cols),
        out_shape=(
            jax.ShapeDtypeStruct((pixels, tile_cols), BF16),
            jax.ShapeDtypeStruct((2, channels * DMAX // LANES, tile_rows, LANES), BF16),
        ),
        in_specs=[VMEM_SPEC, VMEM_SPEC],
        out_specs=(VMEM_SPEC, VMEM_SPEC),
        name="average",
    )(got, second)
    rim = rim_of(averaged.reshape(channels, tile_rows, tile_cols), packs, DMAX, 2)

    out = pl.pallas_call(
        functools.partial(last_kernel, tile_rows, tile_cols),
        out_shape=jax.ShapeDtypeStruct((pixels, tile_cols), BF16),
        in_specs=[SMEM_SPEC] + [VMEM_SPEC] * 8,
        out_specs=VMEM_SPEC,
        scratch_shapes=[
            pltpu.VMEM((wide // LANES, channels * mid_rows, LANES), F32),
            pltpu.VMEM((mid_rows, channels, wide), BF16),
            pltpu.VMEM((tile_cols // LANES, pixels, LANES), F32),
            pltpu.VMEM((1, 3 * hid, 3 * channels), BF16),
        ],
        compiler_params=params,
        name="last_block",
    )(dilations, averaged, *rim, conv_weight, conv_gain, conv_shift, out_weight)
    return out.reshape(channels, tile_rows, tile_cols)


def solution(mesh):
    return jax.shard_map(
        on_device,
        mesh=mesh,
        in_specs=(P(None, "row", "col"), P(), P(), P(), P(), P()),
        out_specs=P(None, "row", "col"),
        check_vma=False,
    )
```

```python
import functools

import jax
import jax.numpy as jnp
from jax import lax
from jax.experimental import pallas as pl
from jax.experimental.pallas import tpu as pltpu
from jax.sharding import PartitionSpec as P

DMAX = 8
LANES = 128
ROWS = 4
PAD = 8
TURN_FIRST = True
F32 = jnp.float32
BF16 = jnp.bfloat16
VMEM_SPEC = pl.BlockSpec(memory_space=pltpu.VMEM)
SMEM_SPEC = pl.BlockSpec(memory_space=pltpu.SMEM)


def pack_sides(x_ref, packs_ref, tile_rows, width):
    per = LANES // width
    last = x_ref.shape[1] - LANES
    lane = lax.broadcasted_iota(jnp.int32, (tile_rows, LANES), 1)

    @pl.loop(0, packs_ref.shape[1])
    def _(g):
        left = right = None
        for j in range(per):
            start = pl.multiple_of((g * per + j) * tile_rows, tile_rows)
            rows = pl.ds(start, tile_rows)
            first = pltpu.roll(x_ref[rows, :LANES].astype(F32), width * j, 1) if j else x_ref[rows, :LANES].astype(F32)
            final = pltpu.roll(
                x_ref[rows, last:].astype(F32), (width * (j + 1)) % LANES, 1
            ) if (width * (j + 1)) % LANES else x_ref[rows, last:].astype(F32)
            here = lane >= width * j
            left = first if left is None else jnp.where(here, first, left)
            right = final if right is None else jnp.where(here, final, right)
        packs_ref[0, g] = left.astype(BF16)
        packs_ref[1, g] = right.astype(BF16)


def pack_kernel(tile_rows, width, x_ref, packs_ref):
    pack_sides(x_ref, packs_ref, tile_rows, width)


DIRECTIONS = [(1, 0), (-1, 0), (0, 1), (0, -1), (1, 1), (1, -1), (-1, 1), (-1, -1)]


def rim_kernel(width, x, packs, vert, side, corner, send_sem, recv_sem):
    rows = x.shape[1]
    here = (lax.axis_index("row"), lax.axis_index("col"))
    counts = (lax.axis_size("row"), lax.axis_size("col"))
    barrier = pltpu.get_barrier_semaphore()

    def exists(step):
        ok = None
        for at, count, d in zip(here, counts, step):
            if d:
                one = at < count - 1 if d > 0 else at > 0
                ok = one if ok is None else jnp.logical_and(ok, one)
        return ok

    def copy(n):
        dr, dc = DIRECTIONS[n]
        edge = pl.ds(rows - width, width) if dr > 0 else pl.ds(0, width)
        tall, broad = (0 if dr > 0 else 1), (0 if dc > 0 else 1)
        if dc == 0:
            src, dst = x.at[:, edge, :], vert.at[tall]
        elif dr == 0:
            src, dst = packs.at[1 - broad], side.at[broad]
        else:
            src, dst = packs.at[1 - broad, :, edge, :], corner.at[tall, broad]
        return pltpu.make_async_remote_copy(
            src_ref=src,
            dst_ref=dst,
            send_sem=send_sem.at[n],
            recv_sem=recv_sem.at[n],
            device_id=(here[0] + dr, here[1] + dc),
            device_id_type=pl.DeviceIdType.MESH,
        )

    total = jnp.int32(0)
    for step in DIRECTIONS:
        near = exists(step)
        total = total + jnp.where(near, 1, 0)

        @pl.when(near)
        def _():
            pl.semaphore_signal(
                barrier,
                inc=1,
                device_id=(here[0] + step[0], here[1] + step[1]),
                device_id_type=pl.DeviceIdType.MESH,
            )

    pl.semaphore_wait(barrier, total)
    for n, step in enumerate(DIRECTIONS):
        @pl.when(exists(step))
        def _():
            copy(n).start()

    for n, step in enumerate(DIRECTIONS):
        @pl.when(exists((-step[0], -step[1])))
        def _():
            copy(n).wait_recv()

        @pl.when(exists(step))
        def _():
            copy(n).wait_send()


def rim_of(x, packs, width, collective_id):
    channels, rows, cols = x.shape
    groups = packs.shape[1]
    anywhere = pl.BlockSpec(memory_space=pl.ANY)
    return pl.pallas_call(
        functools.partial(rim_kernel, width),
        out_shape=(
            jax.ShapeDtypeStruct((2, channels, width, cols), BF16),
            jax.ShapeDtypeStruct((2, groups, rows, LANES), BF16),
            jax.ShapeDtypeStruct((2, 2, groups, width, LANES), BF16),
        ),
        in_specs=[anywhere] * 2,
        out_specs=(anywhere,) * 3,
        scratch_shapes=[pltpu.SemaphoreType.DMA((8,)), pltpu.SemaphoreType.DMA((8,))],
        compiler_params=pltpu.CompilerParams(collective_id=collective_id, has_side_effects=True),
        name="rim_%d" % width,
    )(x, packs)


def conv_rows(src_ref, i, count, groups_out, s, w, gain, shift, expand):
    zero = jnp.zeros((), BF16)
    width = src_ref.shape[2]
    groups = width // LANES
    hid = gain.shape[0]
    centers = [src_ref[i + r + DMAX] for r in range(count)]
    stacked = jnp.concatenate(
        [
            jnp.concatenate([src_ref[i + r + DMAX - s], centers[r], src_ref[i + r + DMAX + s]], axis=0)
            for r in range(count)
        ],
        axis=1,
    )
    taps = jnp.dot(w, jnp.maximum(stacked, zero), preferred_element_type=F32)
    lane = lax.broadcasted_iota(jnp.int32, (hid, LANES), 1)
    from_left, from_right = lane >= s, lane < LANES - s
    hidden = []
    for r in range(count):
        piece = [taps[:, r * width + m * LANES : r * width + (m + 1) * LANES] for m in range(groups)]
        low = [pltpu.roll(y[:hid], s, 1) for y in piece]
        high = [pltpu.roll(y[2 * hid :], LANES - s, 1) for y in piece]
        for m in range(groups_out):
            conv = (
                jnp.where(from_left, low[m], low[m - 1])
                + piece[m][hid : 2 * hid]
                + jnp.where(from_right, high[m], high[(m + 1) % groups])
            )
            hidden.append(jnp.maximum(gain * conv + shift, 0.0).astype(BF16))
    added = lax.dot_general(
        expand, jnp.concatenate(hidden, axis=1), (((0,), (0,)), ((), ())), preferred_element_type=F32
    )
    return [
        [
            centers[r][:, m * LANES : (m + 1) * LANES].astype(F32)
            + added[:, (r * groups_out + m) * LANES : (r * groups_out + m + 1) * LANES]
            for m in range(groups_out)
        ]
        for r in range(count)
    ]


def spread(x_ref, vert, side, corner, wide, by_row, rows, width):
    channels = x_ref.shape[0] // rows
    pitch = wide.shape[1] // channels
    per = LANES // width
    row, col = lax.axis_index("row"), lax.axis_index("col")
    has_up, has_down = row > 0, row < lax.axis_size("row") - 1
    has_left, has_right = col > 0, col < lax.axis_size("col") - 1
    groups = wide.shape[0] - 1

    def filled(height, left, right, j, keep):
        lane = lax.broadcasted_iota(jnp.int32, (height, LANES), 1)
        to_right = (-(j * width)) % LANES
        to_left = (LANES - width - j * width) % LANES
        right = pltpu.roll(right, to_right, 1) if to_right else right
        left = pltpu.roll(left, to_left, 1) if to_left else left
        below = jnp.where(has_right & keep, width, 0)
        above = jnp.where(has_left & keep, LANES - width, LANES)
        return jnp.where(lane < below, right, jnp.where(lane >= above, left, 0.0))

    def kept(value, keep):
        lane = lax.broadcasted_iota(jnp.int32, value.shape, 1)
        return jnp.where(lane < jnp.where(keep, LANES, 0), value, 0.0)

    @pl.loop(0, side.shape[1])
    def _(g):
        for j in range(per):
            c = g * per + j
            start = pl.multiple_of(c * pitch, 8)
            top = pl.ds(start, width)
            middle = pl.ds(pl.multiple_of(start + width, 8), rows)
            bottom = pl.ds(pl.multiple_of(start + width + rows, 8), width)
            inside = pl.ds(pl.multiple_of(c * rows, rows), rows)
            for m in range(groups):
                lanes = slice(m * LANES, (m + 1) * LANES)
                wide[m, middle, :] = x_ref[inside, lanes].astype(F32)
                wide[m, top, :] = kept(vert[0, c, :, lanes].astype(F32), has_up)
                wide[m, bottom, :] = kept(vert[1, c, :, lanes].astype(F32), has_down)
            always = row >= 0
            wide[groups, middle, :] = filled(
                rows, side[0, g].astype(F32), side[1, g].astype(F32), j, always
            )
            wide[groups, top, :] = filled(
                width, corner[0, 0, g].astype(F32), corner[0, 1, g].astype(F32), j, has_up
            )
            wide[groups, bottom, :] = filled(
                width, corner[1, 0, g].astype(F32), corner[1, 1, g].astype(F32), j, has_down
            )

    @pl.loop(0, rows + 2 * width, unroll=4)
    def _(i):
        for g in range(groups + 1):
            by_row[i, :, g * LANES : (g + 1) * LANES] = wide[
                g, pl.ds(i, channels, stride=pitch), :
            ].astype(BF16)


def upright(ref, k):
    hid = ref.shape[1]
    across = jnp.broadcast_to(ref[k : k + 1, :], (hid, hid))
    same = lax.broadcasted_iota(jnp.int32, (hid, hid), 0) == lax.broadcasted_iota(jnp.int32, (hid, hid), 1)
    return jnp.sum(jnp.where(same, across, 0.0), axis=1, keepdims=True)


def stack_weights(w_ref, k, stacked):
    hid, channels = w_ref.shape[2:]
    for p in range(3):
        for q in range(3):
            stacked[q * hid : (q + 1) * hid, p * channels : (p + 1) * channels] = w_ref[k, 3 * p + q]


def first_kernel(
    tile_rows, tile_cols, dil, x_ref, vert, side, corner, w_ref, gain_ref, shift_ref, expand_ref,
    f2_ref, turned_ref, wide, by_row, first, second, taps
):
    mid_rows = tile_rows + 2 * DMAX
    width = by_row.shape[2]
    channels = expand_ref.shape[2]
    spread(x_ref, vert, side, corner, wide, by_row, tile_rows, 2 * DMAX)
    row_base = lax.axis_index("row") * tile_rows - DMAX
    total_rows = lax.axis_size("row") * tile_rows
    lane = lax.broadcasted_iota(jnp.int32, (channels, width), 1)
    col = lax.axis_index("col") * tile_cols + jnp.where(lane < tile_cols + LANES // 2, lane, lane - width)
    col_inside = (col >= 0) & (col < lax.axis_size("col") * tile_cols)
    col_mask = jnp.where(col_inside, 1.0, 0.0).astype(F32)

    s0 = dil[0]
    stack_weights(w_ref, 0, taps.at[0])
    stack_weights(w_ref, 1, taps.at[1])
    gain0, shift0 = upright(gain_ref, 0), upright(shift_ref, 0)
    gain1, shift1 = upright(gain_ref, 1), upright(shift_ref, 1)

    @pl.loop(0, mid_rows, step=ROWS)
    def _(i):
        rows = conv_rows(by_row, i, ROWS, width // LANES, s0, taps[0], gain0, shift0, expand_ref[0])
        for r, pieces in enumerate(rows):
            row = row_base + i + r
            inside = jnp.where((row >= 0) & (row < total_rows), 1.0, 0.0).astype(F32)
            for m, value in enumerate(pieces):
                lanes = slice(m * LANES, (m + 1) * LANES)
                first[i + r, :, lanes] = (value * (col_mask[:, lanes] * inside)).astype(BF16)

    s1 = dil[1]

    @pl.loop(0, tile_rows, step=ROWS)
    def _(i):
        rows = conv_rows(first, i, ROWS, tile_cols // LANES, s1, taps[1], gain1, shift1, expand_ref[1])
        for r, pieces in enumerate(rows):
            for m, value in enumerate(pieces):
                second[m, pl.ds(i + r, channels, stride=tile_rows + PAD), :] = value

    for chunk in range(channels * tile_rows // LANES):
        at = slice(chunk * LANES, (chunk + 1) * LANES)
        for g in range(second.shape[0]):
            across = slice(g * LANES, (g + 1) * LANES)
            per = LANES // tile_rows
            block = jnp.concatenate(
                [
                    second[g, (chunk * per + c) * (tile_rows + PAD) : (chunk * per + c) * (tile_rows + PAD) + tile_rows, :]
                    for c in range(per)
                ],
                axis=0,
            )
            f2_ref[at, across] = block.astype(BF16)
            turned_ref[across, at] = block.T.astype(BF16)


def last_kernel(
    tile_rows, tile_cols, dil, x_ref, vert, side, corner, w_ref, gain_ref, shift_ref, expand_ref,
    out_ref, wide, by_row, second, taps
):
    channels = expand_ref.shape[2]
    spread(x_ref, vert, side, corner, wide, by_row, tile_rows, DMAX)
    s = dil[2]
    stack_weights(w_ref, 2, taps.at[0])
    gain, shift = upright(gain_ref, 2), upright(shift_ref, 2)

    @pl.loop(0, tile_rows, step=ROWS)
    def _(i):
        rows = conv_rows(by_row, i, ROWS, tile_cols // LANES, s, taps[0], gain, shift, expand_ref[2])
        for r, pieces in enumerate(rows):
            for m, value in enumerate(pieces):
                second[m, pl.ds(i + r, channels, stride=tile_rows + PAD), :] = value

    for g in range(second.shape[0]):
        for c in range(channels):
            out_ref[c * tile_rows : (c + 1) * tile_rows, g * LANES : (g + 1) * LANES] = second[
                g, c * (tile_rows + PAD) : c * (tile_rows + PAD) + tile_rows, :
            ].astype(BF16)


def exchange_kernel(group, sent, got, hold, send_sem, recv_sem, send_half, recv_half, hold_sem, pass_sem, local_sem):
    row, col = lax.axis_index("row"), lax.axis_index("col")
    cols = lax.axis_size("col")
    mine, there = row % group, row // group
    on_diagonal = there == col
    off_diagonal = jnp.logical_not(on_diagonal)
    half = sent.shape[1] // 2
    near, far = pl.ds(0, half), pl.ds(half, half)
    mesh_id = pl.DeviceIdType.MESH
    barrier = pltpu.get_barrier_semaphore()
    order = [(mine + d) % group for d in range(group)]

    def partner(k):
        return (col * group + k, there)

    def remote(src, dst, send, recv, device):
        return pltpu.make_async_remote_copy(
            src_ref=src, dst_ref=dst, send_sem=send, recv_sem=recv, device_id=device, device_id_type=mesh_id
        )

    def whole(k, slot):
        return remote(sent.at[k], got.at[slot], send_sem.at[k], recv_sem.at[slot], partner(k))

    def direct(k, slot):
        return remote(sent.at[k, near], got.at[slot, near], send_sem.at[k], recv_sem.at[slot], partner(k))

    def relayed(k):
        device, slot = ((row, there), col * group + k) if TURN_FIRST else ((col * group + k, col), row)
        return remote(sent.at[k, far], hold.at[slot], send_half.at[k], hold_sem.at[slot], device)

    def passed(q):
        device, slot = ((q, col), mine) if TURN_FIRST else ((row, q // group), q % group)
        return remote(hold.at[q], got.at[slot, far], pass_sem.at[q], recv_half.at[slot], device)

    def held(q):
        return remote(hold.at[q], hold.at[q], pass_sem.at[q], hold_sem.at[q], partner((mine + 1) % group))

    def landed(k):
        return remote(hold.at[0], got.at[k, far], send_half.at[k], recv_half.at[k], partner(k))

    def greet(device):
        pl.semaphore_signal(barrier, inc=1, device_id=device, device_id_type=mesh_id)

    through = [((col + e) % cols * group + (mine + d) % group) for d in range(group) for e in range(1, cols)]
    for k in order[1:]:
        greet(partner(k))

    @pl.when(on_diagonal)
    def _():
        for q in through:
            greet((q, col))
        for e in range(1, cols):
            greet((row, (col + e) % cols))

    @pl.when(off_diagonal)
    def _():
        greet(partner(mine))
        for k in order:
            greet((col * group + k, col))
        greet((row, there))

    pl.semaphore_wait(
        barrier, jnp.where(on_diagonal, group - 1 + (cols - 1) * (group + 1), 2 * group + 1)
    )

    @pl.when(off_diagonal)
    def _():
        for k in order:
            relayed(k).start()
            direct(k, mine).start()
        for k in order:
            direct(k, k).wait_recv()
            landed(k).wait_recv()
        for k in order:
            direct(k, mine).wait_send()
            relayed(k).wait_send()

    @pl.when(on_diagonal)
    def _():
        own = pltpu.make_async_copy(sent.at[mine], got.at[mine], local_sem)
        own.start()
        for k in order[1:]:
            whole(k, mine).start()
        for q in through:
            held(q).wait_recv()
            passed(q).start()
        for k in order[1:]:
            whole(k, k).wait_recv()
            whole(k, mine).wait_send()
        for q in through:
            passed(q).wait_send()
        own.wait()


def average_kernel(tile_rows, tile_cols, got, f2_ref, out_ref, packs_ref):
    per = LANES // tile_rows
    lane = lax.broadcasted_iota(jnp.int32, (tile_rows, LANES), 1) // tile_rows
    for g in range(got.shape[2] // LANES):
        for h in range(tile_cols // LANES):
            parts = [
                got[per * h + k, :, g * LANES : (g + 1) * LANES].astype(F32) for k in range(per)
            ]
            for cc in range(per):
                value = None
                for k in range(per):
                    shift = (tile_rows * (k - cc)) % LANES
                    moved = pltpu.roll(parts[k], shift, 1) if shift else parts[k]
                    value = moved if value is None else jnp.where(lane == k, moved, value)
                c = g * per + cc
                at = (slice(c * tile_rows, (c + 1) * tile_rows), slice(h * LANES, (h + 1) * LANES))
                out_ref[at] = (0.5 * (f2_ref[at].astype(F32) + value)).astype(BF16)

    pack_sides(out_ref, packs_ref, tile_rows, DMAX)


def on_device(contact_map, dilations, conv_weight, conv_gain, conv_shift, out_weight):
    channels, tile_rows, tile_cols = contact_map.shape
    blocks, _, hid, _ = conv_weight.shape
    group = tile_cols // tile_rows
    wide = tile_cols + LANES
    deep_rows, mid_rows = tile_rows + 4 * DMAX, tile_rows + 2 * DMAX
    params = pltpu.CompilerParams(vmem_limit_bytes=60000 * 1024)
    pixels = tile_rows * channels

    flat = contact_map.reshape(pixels, tile_cols)
    packs = pl.pallas_call(
        functools.partial(pack_kernel, tile_rows, 2 * DMAX),
        out_shape=jax.ShapeDtypeStruct((2, channels * 2 * DMAX // LANES, tile_rows, LANES), BF16),
        in_specs=[VMEM_SPEC],
        out_specs=VMEM_SPEC,
        name="pack",
    )(flat)
    deep = rim_of(contact_map, packs, 2 * DMAX, 1)
    second, turned = pl.pallas_call(
        functools.partial(first_kernel, tile_rows, tile_cols),
        out_shape=(
            jax.ShapeDtypeStruct((pixels, tile_cols), BF16),
            jax.ShapeDtypeStruct((tile_cols, pixels), BF16),
        ),
        in_specs=[SMEM_SPEC] + [VMEM_SPEC] * 8,
        out_specs=(VMEM_SPEC, VMEM_SPEC),
        scratch_shapes=[
            pltpu.VMEM((wide // LANES, channels * (deep_rows + PAD), LANES), F32),
            pltpu.VMEM((deep_rows, channels, wide), BF16),
            pltpu.VMEM((mid_rows, channels, wide), BF16),
            pltpu.VMEM((tile_cols // LANES, channels * (tile_rows + PAD), LANES), F32),
            pltpu.VMEM((2, 3 * hid, 3 * channels), BF16),
        ],
        compiler_params=params,
        name="first_blocks",
    )(dilations, flat, *deep, conv_weight, conv_gain, conv_shift, out_weight.transpose(0, 2, 1))

    got = pl.pallas_call(
        functools.partial(exchange_kernel, group),
        out_shape=jax.ShapeDtypeStruct((group, tile_rows, pixels), BF16),
        in_specs=[VMEM_SPEC],
        out_specs=VMEM_SPEC,
        scratch_shapes=[pltpu.VMEM((lax.axis_size("row"), tile_rows // 2, pixels), BF16)]
        + [pltpu.SemaphoreType.DMA((group,))] * 4
        + [pltpu.SemaphoreType.DMA((lax.axis_size("row"),))] * 2
        + [pltpu.SemaphoreType.DMA],
        compiler_params=pltpu.CompilerParams(collective_id=0, has_side_effects=True),
        name="exchange",
    )(turned.reshape(group, tile_rows, pixels))

    averaged, packs = pl.pallas_call(
        functools.partial(average_kernel, tile_rows, tile_cols),
        out_shape=(
            jax.ShapeDtypeStruct((pixels, tile_cols), BF16),
            jax.ShapeDtypeStruct((2, channels * DMAX // LANES, tile_rows, LANES), BF16),
        ),
        in_specs=[VMEM_SPEC, VMEM_SPEC],
        out_specs=(VMEM_SPEC, VMEM_SPEC),
        name="average",
    )(got, second)
    rim = rim_of(averaged.reshape(channels, tile_rows, tile_cols), packs, DMAX, 2)

    out = pl.pallas_call(
        functools.partial(last_kernel, tile_rows, tile_cols),
        out_shape=jax.ShapeDtypeStruct((pixels, tile_cols), BF16),
        in_specs=[SMEM_SPEC] + [VMEM_SPEC] * 8,
        out_specs=VMEM_SPEC,
        scratch_shapes=[
            pltpu.VMEM((wide // LANES, channels * (mid_rows + PAD), LANES), F32),
            pltpu.VMEM((mid_rows, channels, wide), BF16),
            pltpu.VMEM((tile_cols // LANES, channels * (tile_rows + PAD), LANES), F32),
            pltpu.VMEM((1, 3 * hid, 3 * channels), BF16),
        ],
        compiler_params=params,
        name="last_block",
    )(dilations, averaged, *rim, conv_weight, conv_gain, conv_shift, out_weight.transpose(0, 2, 1))
    return out.reshape(channels, tile_rows, tile_cols)


def solution(mesh):
    return jax.shard_map(
        on_device,
        mesh=mesh,
        in_specs=(P(None, "row", "col"), P(), P(), P(), P(), P()),
        out_specs=P(None, "row", "col"),
        check_vma=False,
    )
```

```python
import functools

import jax
import jax.numpy as jnp
from jax import lax
from jax.experimental import pallas as pl
from jax.experimental.pallas import tpu as pltpu
from jax.sharding import PartitionSpec as P

DMAX = 8
LANES = 128
ROWS = 8
PAD = 8
TURN_FIRST = True
F32 = jnp.float32
BF16 = jnp.bfloat16
VMEM_SPEC = pl.BlockSpec(memory_space=pltpu.VMEM)
SMEM_SPEC = pl.BlockSpec(memory_space=pltpu.SMEM)


def pack_sides(x_ref, packs_ref, tile_rows, width):
    per = LANES // width
    last = x_ref.shape[1] - LANES
    lane = lax.broadcasted_iota(jnp.int32, (tile_rows, LANES), 1)

    @pl.loop(0, packs_ref.shape[1])
    def _(g):
        left = right = None
        for j in range(per):
            start = pl.multiple_of((g * per + j) * tile_rows, tile_rows)
            rows = pl.ds(start, tile_rows)
            first = pltpu.roll(x_ref[rows, :LANES].astype(F32), width * j, 1) if j else x_ref[rows, :LANES].astype(F32)
            final = pltpu.roll(
                x_ref[rows, last:].astype(F32), (width * (j + 1)) % LANES, 1
            ) if (width * (j + 1)) % LANES else x_ref[rows, last:].astype(F32)
            here = lane >= width * j
            left = first if left is None else jnp.where(here, first, left)
            right = final if right is None else jnp.where(here, final, right)
        packs_ref[0, g] = left.astype(BF16)
        packs_ref[1, g] = right.astype(BF16)


DIRECTIONS = [(1, 0), (-1, 0), (0, 1), (0, -1), (1, 1), (1, -1), (-1, 1), (-1, -1)]


def rim_kernel(width, x, flat, vert, side, corner, packs, send_sem, recv_sem):
    rim_steps(width, x, packs, vert, side, corner, send_sem, recv_sem, flat)


def rim_steps(width, x, packs, vert, side, corner, send_sem, recv_sem, flat=None):
    rows = x.shape[1]
    here = (lax.axis_index("row"), lax.axis_index("col"))
    counts = (lax.axis_size("row"), lax.axis_size("col"))
    barrier = pltpu.get_barrier_semaphore()

    def exists(step):
        ok = None
        for at, count, d in zip(here, counts, step):
            if d:
                one = at < count - 1 if d > 0 else at > 0
                ok = one if ok is None else jnp.logical_and(ok, one)
        return ok

    def copy(n):
        dr, dc = DIRECTIONS[n]
        edge = pl.ds(rows - width, width) if dr > 0 else pl.ds(0, width)
        tall, broad = (0 if dr > 0 else 1), (0 if dc > 0 else 1)
        if dc == 0:
            src, dst = x.at[:, edge, :], vert.at[tall]
        elif dr == 0:
            src, dst = packs.at[1 - broad], side.at[broad]
        else:
            src, dst = packs.at[1 - broad, :, edge, :], corner.at[tall, broad]
        return pltpu.make_async_remote_copy(
            src_ref=src,
            dst_ref=dst,
            send_sem=send_sem.at[n],
            recv_sem=recv_sem.at[n],
            device_id=(here[0] + dr, here[1] + dc),
            device_id_type=pl.DeviceIdType.MESH,
        )

    total = jnp.int32(0)
    for step in DIRECTIONS:
        near = exists(step)
        total = total + jnp.where(near, 1, 0)

        @pl.when(near)
        def _():
            pl.semaphore_signal(
                barrier,
                inc=1,
                device_id=(here[0] + step[0], here[1] + step[1]),
                device_id_type=pl.DeviceIdType.MESH,
            )

    pl.semaphore_wait(barrier, total)
    for n, step in enumerate(DIRECTIONS):
        if n == 2 and flat is not None:
            pack_sides(flat, packs, rows, width)

        @pl.when(exists(step))
        def _():
            copy(n).start()

    for n, step in enumerate(DIRECTIONS):
        @pl.when(exists((-step[0], -step[1])))
        def _():
            copy(n).wait_recv()

        @pl.when(exists(step))
        def _():
            copy(n).wait_send()


def rim_of(x, packs, width, collective_id, flat=None):
    channels, rows, cols = x.shape
    groups = channels * width // LANES
    semaphores = [pltpu.SemaphoreType.DMA((8,)), pltpu.SemaphoreType.DMA((8,))]
    room = [] if flat is None else [pltpu.VMEM((2, groups, rows, LANES), BF16)]
    anywhere = pl.BlockSpec(memory_space=pl.ANY)
    return pl.pallas_call(
        functools.partial(rim_steps if flat is None else rim_kernel, width),
        out_shape=(
            jax.ShapeDtypeStruct((2, channels, width, cols), BF16),
            jax.ShapeDtypeStruct((2, groups, rows, LANES), BF16),
            jax.ShapeDtypeStruct((2, 2, groups, width, LANES), BF16),
        ),
        in_specs=[anywhere, anywhere if flat is None else VMEM_SPEC],
        out_specs=(anywhere,) * 3,
        scratch_shapes=room + semaphores,
        compiler_params=pltpu.CompilerParams(collective_id=collective_id, has_side_effects=True),
        name="rim_%d" % width,
    )(x, packs if flat is None else flat)


def conv_rows(src_ref, i, count, groups_out, s, w, gain, shift, expand):
    zero = jnp.zeros((), BF16)
    width = src_ref.shape[2]
    groups = width // LANES
    hid = gain.shape[0]
    centers = [src_ref[i + r + DMAX] for r in range(count)]
    stacked = jnp.concatenate(
        [
            jnp.concatenate([src_ref[i + r + DMAX - s], centers[r], src_ref[i + r + DMAX + s]], axis=0)
            for r in range(count)
        ],
        axis=1,
    )
    taps = jnp.dot(w, jnp.maximum(stacked, zero), preferred_element_type=F32)
    lane = lax.broadcasted_iota(jnp.int32, (hid, LANES), 1)
    from_left, from_right = lane >= s, lane < LANES - s
    hidden = []
    for r in range(count):
        piece = [taps[:, r * width + m * LANES : r * width + (m + 1) * LANES] for m in range(groups)]
        low = [pltpu.roll(y[:hid], s, 1) for y in piece]
        high = [pltpu.roll(y[2 * hid :], LANES - s, 1) for y in piece]
        for m in range(groups_out):
            conv = (
                jnp.where(from_left, low[m], low[m - 1])
                + piece[m][hid : 2 * hid]
                + jnp.where(from_right, high[m], high[(m + 1) % groups])
            )
            hidden.append(jnp.maximum(gain * conv + shift, 0.0).astype(BF16))
    added = lax.dot_general(
        expand, jnp.concatenate(hidden, axis=1), (((0,), (0,)), ((), ())), preferred_element_type=F32
    )
    return [
        [
            centers[r][:, m * LANES : (m + 1) * LANES].astype(F32)
            + added[:, (r * groups_out + m) * LANES : (r * groups_out + m + 1) * LANES]
            for m in range(groups_out)
        ]
        for r in range(count)
    ]


def spread(x_ref, vert, side, corner, wide, by_row, rows, width):
    channels = x_ref.shape[0] // rows
    pitch = wide.shape[1] // channels
    per = LANES // width
    row, col = lax.axis_index("row"), lax.axis_index("col")
    has_up, has_down = row > 0, row < lax.axis_size("row") - 1
    has_left, has_right = col > 0, col < lax.axis_size("col") - 1
    groups = wide.shape[0] - 1

    def filled(height, left, right, j, keep):
        lane = lax.broadcasted_iota(jnp.int32, (height, LANES), 1)
        to_right = (-(j * width)) % LANES
        to_left = (LANES - width - j * width) % LANES
        right = pltpu.roll(right, to_right, 1) if to_right else right
        left = pltpu.roll(left, to_left, 1) if to_left else left
        below = jnp.where(has_right & keep, width, 0)
        above = jnp.where(has_left & keep, LANES - width, LANES)
        return jnp.where(lane < below, right, jnp.where(lane >= above, left, 0.0))

    def kept(value, keep):
        lane = lax.broadcasted_iota(jnp.int32, value.shape, 1)
        return jnp.where(lane < jnp.where(keep, LANES, 0), value, 0.0)

    @pl.loop(0, side.shape[1], unroll=2)
    def _(g):
        for j in range(per):
            c = g * per + j
            start = pl.multiple_of(c * pitch, 8)
            top = pl.ds(start, width)
            middle = pl.ds(pl.multiple_of(start + width, 8), rows)
            bottom = pl.ds(pl.multiple_of(start + width + rows, 8), width)
            inside = pl.ds(pl.multiple_of(c * rows, rows), rows)
            for m in range(groups):
                lanes = slice(m * LANES, (m + 1) * LANES)
                wide[m, middle, :] = x_ref[inside, lanes].astype(F32)
                wide[m, top, :] = kept(vert[0, c, :, lanes].astype(F32), has_up)
                wide[m, bottom, :] = kept(vert[1, c, :, lanes].astype(F32), has_down)
            always = row >= 0
            wide[groups, middle, :] = filled(
                rows, side[0, g].astype(F32), side[1, g].astype(F32), j, always
            )
            wide[groups, top, :] = filled(
                width, corner[0, 0, g].astype(F32), corner[0, 1, g].astype(F32), j, has_up
            )
            wide[groups, bottom, :] = filled(
                width, corner[1, 0, g].astype(F32), corner[1, 1, g].astype(F32), j, has_down
            )

    @pl.loop(0, rows + 2 * width, unroll=8)
    def _(i):
        for g in range(groups + 1):
            by_row[i, :, g * LANES : (g + 1) * LANES] = wide[
                g, pl.ds(i, channels, stride=pitch), :
            ].astype(BF16)


def upright(ref, k):
    hid = ref.shape[1]
    across = jnp.broadcast_to(ref[k : k + 1, :], (hid, hid))
    same = lax.broadcasted_iota(jnp.int32, (hid, hid), 0) == lax.broadcasted_iota(jnp.int32, (hid, hid), 1)
    return jnp.sum(jnp.where(same, across, 0.0), axis=1, keepdims=True)


def stack_weights(w_ref, k, stacked):
    hid, channels = w_ref.shape[2:]
    for p in range(3):
        for q in range(3):
            stacked[q * hid : (q + 1) * hid, p * channels : (p + 1) * channels] = w_ref[k, 3 * p + q]


def first_kernel(
    tile_rows, tile_cols, dil, x_ref, vert, side, corner, w_ref, gain_ref, shift_ref, expand_ref,
    f2_ref, turned_ref, wide, by_row, first, second, taps
):
    mid_rows = tile_rows + 2 * DMAX
    width = by_row.shape[2]
    channels = expand_ref.shape[2]
    spread(x_ref, vert, side, corner, wide, by_row, tile_rows, 2 * DMAX)
    row_base = lax.axis_index("row") * tile_rows - DMAX
    total_rows = lax.axis_size("row") * tile_rows
    lane = lax.broadcasted_iota(jnp.int32, (channels, width), 1)
    col = lax.axis_index("col") * tile_cols + jnp.where(lane < tile_cols + LANES // 2, lane, lane - width)
    col_inside = (col >= 0) & (col < lax.axis_size("col") * tile_cols)
    col_mask = jnp.where(col_inside, 1.0, 0.0).astype(F32)

    s0 = dil[0]
    stack_weights(w_ref, 0, taps.at[0])
    stack_weights(w_ref, 1, taps.at[1])
    gain0, shift0 = upright(gain_ref, 0), upright(shift_ref, 0)
    gain1, shift1 = upright(gain_ref, 1), upright(shift_ref, 1)

    @pl.loop(0, mid_rows, step=ROWS)
    def _(i):
        rows = conv_rows(by_row, i, ROWS, width // LANES, s0, taps[0], gain0, shift0, expand_ref[0])
        for r, pieces in enumerate(rows):
            row = row_base + i + r
            inside = jnp.where((row >= 0) & (row < total_rows), 1.0, 0.0).astype(F32)
            for m, value in enumerate(pieces):
                lanes = slice(m * LANES, (m + 1) * LANES)
                first[i + r, :, lanes] = (value * (col_mask[:, lanes] * inside)).astype(BF16)

    s1 = dil[1]

    @pl.loop(0, tile_rows, step=ROWS)
    def _(i):
        rows = conv_rows(first, i, ROWS, tile_cols // LANES, s1, taps[1], gain1, shift1, expand_ref[1])
        for r, pieces in enumerate(rows):
            for m, value in enumerate(pieces):
                second[m, pl.ds(i + r, channels, stride=tile_rows + PAD), :] = value

    for chunk in range(channels * tile_rows // LANES):
        at = slice(chunk * LANES, (chunk + 1) * LANES)
        for g in range(second.shape[0]):
            across = slice(g * LANES, (g + 1) * LANES)
            per = LANES // tile_rows
            block = jnp.concatenate(
                [
                    second[g, (chunk * per + c) * (tile_rows + PAD) : (chunk * per + c) * (tile_rows + PAD) + tile_rows, :]
                    for c in range(per)
                ],
                axis=0,
            )
            f2_ref[at, across] = block.astype(BF16)
            turned_ref[across, at] = block.T.astype(BF16)


def last_kernel(
    tile_rows, tile_cols, dil, x_ref, vert, side, corner, w_ref, gain_ref, shift_ref, expand_ref,
    out_ref, wide, by_row, second, taps
):
    channels = expand_ref.shape[2]
    spread(x_ref, vert, side, corner, wide, by_row, tile_rows, DMAX)
    s = dil[2]
    stack_weights(w_ref, 2, taps.at[0])
    gain, shift = upright(gain_ref, 2), upright(shift_ref, 2)

    @pl.loop(0, tile_rows, step=ROWS)
    def _(i):
        rows = conv_rows(by_row, i, ROWS, tile_cols // LANES, s, taps[0], gain, shift, expand_ref[2])
        for r, pieces in enumerate(rows):
            for m, value in enumerate(pieces):
                second[m, pl.ds(i + r, channels, stride=tile_rows + PAD), :] = value

    for g in range(second.shape[0]):
        for c in range(channels):
            out_ref[c * tile_rows : (c + 1) * tile_rows, g * LANES : (g + 1) * LANES] = second[
                g, c * (tile_rows + PAD) : c * (tile_rows + PAD) + tile_rows, :
            ].astype(BF16)


def exchange_kernel(group, sent, got, hold, send_sem, recv_sem, send_half, recv_half, hold_sem, pass_sem, local_sem):
    row, col = lax.axis_index("row"), lax.axis_index("col")
    cols = lax.axis_size("col")
    mine, there = row % group, row // group
    on_diagonal = there == col
    off_diagonal = jnp.logical_not(on_diagonal)
    half = sent.shape[1] // 2
    near, far = pl.ds(0, half), pl.ds(half, half)
    mesh_id = pl.DeviceIdType.MESH
    barrier = pltpu.get_barrier_semaphore()
    order = [(mine + d) % group for d in range(group)]

    def partner(k):
        return (col * group + k, there)

    def remote(src, dst, send, recv, device):
        return pltpu.make_async_remote_copy(
            src_ref=src, dst_ref=dst, send_sem=send, recv_sem=recv, device_id=device, device_id_type=mesh_id
        )

    def whole(k, slot):
        return remote(sent.at[k], got.at[slot], send_sem.at[k], recv_sem.at[slot], partner(k))

    def direct(k, slot):
        return remote(sent.at[k, near], got.at[slot, near], send_sem.at[k], recv_sem.at[slot], partner(k))

    def relayed(k):
        device, slot = ((row, there), col * group + k) if TURN_FIRST else ((col * group + k, col), row)
        return remote(sent.at[k, far], hold.at[slot], send_half.at[k], hold_sem.at[slot], device)

    def passed(q):
        device, slot = ((q, col), mine) if TURN_FIRST else ((row, q // group), q % group)
        return remote(hold.at[q], got.at[slot, far], pass_sem.at[q], recv_half.at[slot], device)

    def held(q):
        return remote(hold.at[q], hold.at[q], pass_sem.at[q], hold_sem.at[q], partner((mine + 1) % group))

    def landed(k):
        return remote(hold.at[0], got.at[k, far], send_half.at[k], recv_half.at[k], partner(k))

    def greet(device):
        pl.semaphore_signal(barrier, inc=1, device_id=device, device_id_type=mesh_id)

    through = [((col + e) % cols * group + (mine + d) % group) for d in range(group) for e in range(1, cols)]
    for k in order[1:]:
        greet(partner(k))

    @pl.when(on_diagonal)
    def _():
        for q in through:
            greet((q, col))
        for e in range(1, cols):
            greet((row, (col + e) % cols))

    @pl.when(off_diagonal)
    def _():
        greet(partner(mine))
        for k in order:
            greet((col * group + k, col))
        greet((row, there))

    pl.semaphore_wait(
        barrier, jnp.where(on_diagonal, group - 1 + (cols - 1) * (group + 1), 2 * group + 1)
    )

    @pl.when(off_diagonal)
    def _():
        for k in order:
            relayed(k).start()
            direct(k, mine).start()
        for k in order:
            direct(k, k).wait_recv()
            landed(k).wait_recv()
        for k in order:
            direct(k, mine).wait_send()
            relayed(k).wait_send()

    @pl.when(on_diagonal)
    def _():
        own = pltpu.make_async_copy(sent.at[mine], got.at[mine], local_sem)
        own.start()
        for k in order[1:]:
            whole(k, mine).start()
        for q in through:
            held(q).wait_recv()
            passed(q).start()
        for k in order[1:]:
            whole(k, k).wait_recv()
            whole(k, mine).wait_send()
        for q in through:
            passed(q).wait_send()
        own.wait()


def average_kernel(tile_rows, tile_cols, got, f2_ref, out_ref, packs_ref):
    per = LANES // tile_rows
    lane = lax.broadcasted_iota(jnp.int32, (tile_rows, LANES), 1) // tile_rows
    for g in range(got.shape[2] // LANES):
        for h in range(tile_cols // LANES):
            parts = [
                got[per * h + k, :, g * LANES : (g + 1) * LANES].astype(F32) for k in range(per)
            ]
            for cc in range(per):
                value = None
                for k in range(per):
                    shift = (tile_rows * (k - cc)) % LANES
                    moved = pltpu.roll(parts[k], shift, 1) if shift else parts[k]
                    value = moved if value is None else jnp.where(lane == k, moved, value)
                c = g * per + cc
                at = (slice(c * tile_rows, (c + 1) * tile_rows), slice(h * LANES, (h + 1) * LANES))
                out_ref[at] = (0.5 * (f2_ref[at].astype(F32) + value)).astype(BF16)

    pack_sides(out_ref, packs_ref, tile_rows, DMAX)


def on_device(contact_map, dilations, conv_weight, conv_gain, conv_shift, out_weight):
    channels, tile_rows, tile_cols = contact_map.shape
    blocks, _, hid, _ = conv_weight.shape
    group = tile_cols // tile_rows
    wide = tile_cols + LANES
    deep_rows, mid_rows = tile_rows + 4 * DMAX, tile_rows + 2 * DMAX
    params = pltpu.CompilerParams(vmem_limit_bytes=60000 * 1024)
    pixels = tile_rows * channels

    flat = contact_map.reshape(pixels, tile_cols)
    deep = rim_of(contact_map, None, 2 * DMAX, 1, flat)
    second, turned = pl.pallas_call(
        functools.partial(first_kernel, tile_rows, tile_cols),
        out_shape=(
            jax.ShapeDtypeStruct((pixels, tile_cols), BF16),
            jax.ShapeDtypeStruct((tile_cols, pixels), BF16),
        ),
        in_specs=[SMEM_SPEC] + [VMEM_SPEC] * 8,
        out_specs=(VMEM_SPEC, VMEM_SPEC),
        scratch_shapes=[
            pltpu.VMEM((wide // LANES, channels * (deep_rows + PAD), LANES), F32),
            pltpu.VMEM((deep_rows, channels, wide), BF16),
            pltpu.VMEM((mid_rows, channels, wide), BF16),
            pltpu.VMEM((tile_cols // LANES, channels * (tile_rows + PAD), LANES), F32),
            pltpu.VMEM((2, 3 * hid, 3 * channels), BF16),
        ],
        compiler_params=params,
        name="first_blocks",
    )(dilations, flat, *deep, conv_weight, conv_gain, conv_shift, out_weight.transpose(0, 2, 1))

    got = pl.pallas_call(
        functools.partial(exchange_kernel, group),
        out_shape=jax.ShapeDtypeStruct((group, tile_rows, pixels), BF16),
        in_specs=[VMEM_SPEC],
        out_specs=VMEM_SPEC,
        scratch_shapes=[pltpu.VMEM((lax.axis_size("row"), tile_rows // 2, pixels), BF16)]
        + [pltpu.SemaphoreType.DMA((group,))] * 4
        + [pltpu.SemaphoreType.DMA((lax.axis_size("row"),))] * 2
        + [pltpu.SemaphoreType.DMA],
        compiler_params=pltpu.CompilerParams(collective_id=0, has_side_effects=True),
        name="exchange",
    )(turned.reshape(group, tile_rows, pixels))

    averaged, packs = pl.pallas_call(
        functools.partial(average_kernel, tile_rows, tile_cols),
        out_shape=(
            jax.ShapeDtypeStruct((pixels, tile_cols), BF16),
            jax.ShapeDtypeStruct((2, channels * DMAX // LANES, tile_rows, LANES), BF16),
        ),
        in_specs=[VMEM_SPEC, VMEM_SPEC],
        out_specs=(VMEM_SPEC, VMEM_SPEC),
        name="average",
    )(got, second)
    rim = rim_of(averaged.reshape(channels, tile_rows, tile_cols), packs, DMAX, 2)

    out = pl.pallas_call(
        functools.partial(last_kernel, tile_rows, tile_cols),
        out_shape=jax.ShapeDtypeStruct((pixels, tile_cols), BF16),
        in_specs=[SMEM_SPEC] + [VMEM_SPEC] * 8,
        out_specs=VMEM_SPEC,
        scratch_shapes=[
            pltpu.VMEM((wide // LANES, channels * (mid_rows + PAD), LANES), F32),
            pltpu.VMEM((mid_rows, channels, wide), BF16),
            pltpu.VMEM((tile_cols // LANES, channels * (tile_rows + PAD), LANES), F32),
            pltpu.VMEM((1, 3 * hid, 3 * channels), BF16),
        ],
        compiler_params=params,
        name="last_block",
    )(dilations, averaged, *rim, conv_weight, conv_gain, conv_shift, out_weight.transpose(0, 2, 1))
    return out.reshape(channels, tile_rows, tile_cols)


def solution(mesh):
    return jax.shard_map(
        on_device,
        mesh=mesh,
        in_specs=(P(None, "row", "col"), P(), P(), P(), P(), P()),
        out_specs=P(None, "row", "col"),
        check_vma=False,
    )
```
